32 devices in a mesh: ctx: 8 (over y, x, core), ch: 4 (over z).
Axes of the slice: x: 2, y: 2, z: 4, core: 2. Of those that a mesh axis runs over, the one named last changes fastest.
Arguments:
- query_act: bfloat16 [4096, 4096], P('ctx', 'ch'), may hold values from -6 to 6
- key_act: bfloat16 [4096, 4096], P('ctx', 'ch'), may hold values from -6 to 6
- value_act: bfloat16 [4096, 4096], P('ctx', 'ch'), may hold values from -6 to 6
- filters: bfloat16 [4096, 128], P('ch'), may hold values from -0.5 to 0.5
- proj_weight: bfloat16 [8192, 4096], P('ctx', 'ch'), may hold values from -0.09375 to 0.09375
- cotangent: bfloat16 [4096, 8192], P('ctx', 'ch'), may hold values from -6 to 6
Outputs:
- grad_query: bfloat16 [4096, 4096], P('ctx', 'ch')
- grad_key: bfloat16 [4096, 4096], P('ctx', 'ch')
- grad_value: bfloat16 [4096, 4096], P('ctx', 'ch')
- grad_filter: float32 [4096, 128], P('ch')
- grad_proj: float32 [8192, 4096], P('ctx', 'ch')
The draws below stay inside these ranges and needn't reach their ends.
All inputs are finite; a program needn't handle non-finite values.
Results may differ from the reference program's by a relative error of at most 0.0051.
Values may be sent and summed in bfloat16 or wider, within the bound.
A program may use at most 192 MiB of HBM per device.

```python
import jax
import jax.numpy as jnp
from jax import lax

D = 8192
C = 4096
TAPS = 128
TOKENS = 4096


def strengthened(array, own_key, source, target, shards_of, factor):
    owner, partner = [(jnp.arange(array.shape[axis_at]) // (array.shape[axis_at] // shards_of)).reshape([-1 if axis == axis_at else 1 for axis in range(array.ndim)]) for axis_at in (source, target)]
    chosen = jax.random.permutation(own_key, shards_of)[partner]
    strong = (owner == chosen) | (owner == (partner + shards_of // 2) % shards_of)
    return jnp.where(strong, factor * array, array)


def level_of(stream_key, extent, split, smallest, top_value):
    loudness = 1.0
    for axis_at, blocks in split:
        draws = jax.random.uniform(jax.random.fold_in(jax.random.fold_in(stream_key, 6), axis_at), (blocks,), jnp.float32, smallest / len(split), top_value / len(split))
        loudness = loudness * jnp.repeat(jnp.exp(draws), extent[axis_at] // blocks).reshape((-1,) + (1,) * (len(extent) - 1 - axis_at))
    return loudness


def bell_draw(stream_key, extent, width, most, shards=(), held_as=jnp.bfloat16):
    gain = level_of(stream_key, extent, shards, -0.22, 0.18) if shards else 1.0
    result = jax.random.normal(stream_key, extent, jnp.float32) * width * gain
    return jnp.minimum(jnp.maximum(result, -most), most).astype(held_as)


def bell_draw_with(key, dims, scale, reach, pieces, heavy, held_as=jnp.bfloat16):
    values = scale * jax.random.normal(key, dims, jnp.float32)
    if pieces:
        values = values * level_of(key, dims, pieces, -0.22, 0.18)
    return jnp.clip(strengthened(values, jax.random.fold_in(key, 3), *heavy), -reach, reach).astype(held_as)


def setup_inputs(seed: int = 0) -> dict:
    keys = jax.random.split(jax.random.key(seed), 7)
    return {
        "query_act": bell_draw(keys[0], (TOKENS, C), 1.0, 6.0, ((0, 8), (1, 4))),
        "key_act": bell_draw(keys[1], (TOKENS, C), 1.0, 6.0, ((0, 8), (1, 4))),
        "value_act": bell_draw(keys[2], (TOKENS, C), 1.0, 6.0, ((0, 8), (1, 4))),
        "filters": bell_draw(keys[3], (C, TAPS), TAPS ** -0.5, 0.5, ((0, 4),)),
        "proj_weight": bell_draw(keys[4], (D, C), C ** -0.5, 0.09375, ((0, 8), (1, 4))),
        "cotangent": bell_draw_with(keys[5], (TOKENS, D), 1.0, 6.0, ((0, 8), (1, 4)), (0, 1, 8, 2.0)),
    }


def causal_mix(filt, signal):
    padded = jnp.concatenate([jnp.zeros((TAPS - 1, signal.shape[1]), jnp.float32), signal], 0)

    def add_tap(lag_index, total):
        offset = jnp.int32(TAPS - 1) - lag_index.astype(jnp.int32)
        portion = lax.dynamic_slice_in_dim(padded, offset, signal.shape[0], 0)
        column = lax.dynamic_index_in_dim(filt, lag_index.astype(jnp.int32), 1, keepdims=False)
        return total + column[None, :] * portion

    return lax.fori_loop(0, TAPS, add_tap, jnp.zeros(signal.shape, jnp.float32))


def anti_mix(filt, signal):
    padded = jnp.concatenate([signal, jnp.zeros((TAPS - 1, signal.shape[1]), jnp.float32)], 0)

    def add_tap(lag_index, total):
        offset = lag_index.astype(jnp.int32)
        portion = lax.dynamic_slice_in_dim(padded, offset, signal.shape[0], 0)
        column = lax.dynamic_index_in_dim(filt, lag_index.astype(jnp.int32), 1, keepdims=False)
        return total + column[None, :] * portion

    return lax.fori_loop(0, TAPS, add_tap, jnp.zeros(signal.shape, jnp.float32))


def filter_terms(grad_gate, product):
    padded = jnp.concatenate([jnp.zeros((TAPS - 1, product.shape[1]), jnp.float32), product], 0)

    def one_lag(lag_index):
        offset = jnp.int32(TAPS - 1) - lag_index.astype(jnp.int32)
        portion = lax.dynamic_slice_in_dim(padded, offset, product.shape[0], 0)
        return jnp.sum(grad_gate * portion, axis=0)

    return lax.map(one_lag, jnp.arange(TAPS, dtype=jnp.int32)).T


def reference(query_act, key_act, value_act, filters, proj_weight, cotangent):
    query_f = query_act.astype(jnp.float32)
    key_f = key_act.astype(jnp.float32)
    value_f = value_act.astype(jnp.float32)
    filt = filters.astype(jnp.float32)
    product = (key_f * value_f).astype(jnp.bfloat16)
    product_f = product.astype(jnp.float32)
    mixed = causal_mix(filt, product_f)
    gated = (query_f * mixed).astype(jnp.bfloat16)
    grad_mix = jnp.dot(cotangent, proj_weight, preferred_element_type=jnp.float32)
    grad_query = (grad_mix * mixed).astype(jnp.bfloat16)
    grad_gate = (grad_mix * query_f).astype(jnp.bfloat16)
    grad_gate_f = grad_gate.astype(jnp.float32)
    grad_prod = anti_mix(filt, grad_gate_f)
    grad_key = (grad_prod * value_f).astype(jnp.bfloat16)
    grad_value = (grad_prod * key_f).astype(jnp.bfloat16)
    grad_filter = filter_terms(grad_gate_f, product_f)
    grad_proj = lax.dot_general(cotangent, gated, (((0,), (0,)), ((), ())), preferred_element_type=jnp.float32)
    return (grad_query, grad_key, grad_value, grad_filter, grad_proj)
```

```python
import functools

import jax
import jax.numpy as jnp
import ml_dtypes
import numpy as np
from jax import lax
from jax.experimental import pallas as pl
from jax.experimental.pallas import tpu as pltpu
from jax.sharding import PartitionSpec as P

TAPS = 128
WIDE = 128
TILE = 256
MESH = pl.DeviceIdType.MESH
BF16 = jnp.bfloat16
F32 = jnp.float32


def basis(points):
    freqs = points // 2
    phase = (2 * np.arange(freqs)[:, None] + 1) * np.arange(points)[None, :] % (2 * points)
    angle = np.pi * phase / points
    return np.concatenate([np.cos(angle), np.sin(angle)], 0).astype(np.float32)


def constant_pair(a):
    hi = a.astype(ml_dtypes.bfloat16)
    lo = (a - hi.astype(np.float32)).astype(ml_dtypes.bfloat16)
    return hi, lo


def split(a):
    hi = a.astype(BF16)
    return hi, (a - hi.astype(F32)).astype(BF16)


def dot32(a, b):
    return jnp.dot(a, b, preferred_element_type=F32)


def forward(hi, lo, x):
    return dot32(hi, x) + dot32(lo, x)


def backward(thi, tlo, y):
    yhi, ylo = split(y)
    return dot32(thi, yhi) + dot32(thi, ylo) + dot32(tlo, yhi)


def halves(x):
    n = x.shape[0] // 2
    return x[:n], x[n:]


def times(x, f):
    (xc, xs), (fc, fs) = halves(x), halves(f)
    return jnp.concatenate([xc * fc - xs * fs, xc * fs + xs * fc], 0)


def times_conj(x, f):
    (xc, xs), (fc, fs) = halves(x), halves(f)
    return jnp.concatenate([xc * fc + xs * fs, xs * fc - xc * fs], 0)


def kernel(n_ctx, n_ch, query_in, key_in, value_in, filt_in, weight, cot, thi_in, tlo_in, ihi_in, ilo_in, lhi_in, llo_in,
           g_query, g_key, g_value, g_filter, g_proj,
           blocks, weights, acc, acc_in, query, key, value, filt, thi, tlo, ihi, ilo, lhi, llo,
           prodx, gatex, gated, mix, pspec, fspec,
           a1_out, b1_out, a2_out, b2_out, a1_in, b1_in, a2_in, b2_in, f_out, f_in, f_all,
           load_sem, own_sem, swap_sem, z_send, z_recv, w1_send, w1_recv, w2_send, w2_recv,
           a1_send, a1_recv, b1_send, b1_recv, a2_send, a2_recv, b2_send, b2_recv,
           halo_sem, pair_sem, fs_send, fs_recv, fg_send, fg_recv):
    chips = n_ctx // 2
    ny = chips // 2
    hops = n_ch - 1
    ctx = lax.axis_index("ctx")
    ch = lax.axis_index("ch")
    chip, core = ctx // 2, ctx % 2
    y, x = chip // 2, chip % 2
    other = chip * 2 + 1 - core
    x_chip = y * 2 + 1 - x
    tokens = query.shape[0]
    channels = query.shape[1]
    rows = weight.shape[0]
    chunks = rows // WIDE
    half = channels // 2
    wh = WIDE // 2
    own = pl.multiple_of(core * tokens, tokens)
    theirs = pl.multiple_of((1 - core) * tokens, tokens)

    def device(c):
        return (c * 2 + core, ch)

    def y_at(o):
        return (y + o) % ny

    def remote(src, dst, send, recv, to):
        return pltpu.make_async_remote_copy(src, dst, send, recv, device_id=to, device_id_type=MESH)

    barrier = pltpu.get_barrier_semaphore()
    for off in range(1, n_ctx):
        pl.semaphore_signal(barrier, inc=1, device_id=((ctx + off) % n_ctx, ch), device_id_type=MESH)
    for off in (1, n_ch - 1):
        pl.semaphore_signal(barrier, inc=1, device_id=(ctx, (ch + off) % n_ch), device_id_type=MESH)

    loads = [pltpu.make_async_copy(a, b, load_sem.at[i]) for i, (a, b) in enumerate((
        (key_in, key), (value_in, value), (filt_in, filt), (thi_in, thi), (tlo_in, tlo), (ihi_in, ihi), (ilo_in, ilo),
        (query_in, query), (lhi_in, lhi), (llo_in, llo)))]

    def own_copy(c):
        return pltpu.make_async_copy(
            cot.at[:, pl.ds(pl.multiple_of(core * rows + c * WIDE, WIDE), WIDE)],
            blocks.at[c, ch, pl.ds(own, tokens)], own_sem.at[c])

    def swap_copy(c):
        return remote(
            cot.at[:, pl.ds(pl.multiple_of((1 - core) * rows + c * WIDE, WIDE), WIDE)],
            blocks.at[c, ch, pl.ds(own, tokens)], swap_sem.at[0, c], swap_sem.at[1, c], (other, ch))

    def w_rows(c, q):
        return weights.at[c, pl.ds(pl.multiple_of(q * WIDE, WIDE), WIDE)]

    def w_piece(c):
        return weight.at[pl.ds(pl.multiple_of(c * WIDE, WIDE), WIDE)]

    w_own = [pltpu.make_async_copy(w_piece(c), w_rows(c, chip), load_sem.at[len(loads) + c]) for c in range(chunks)]

    def w1x(c):
        return remote(w_piece(c), w_rows(c, chip), w1_send.at[c, 0], w1_recv.at[c, 0], device(x_chip))

    def w1y(c, o):
        return remote(w_piece(c), w_rows(c, chip), w1_send.at[c, o], w1_recv.at[c, o], device(y_at(o) * 2 + x))

    def w2y(c, o):
        piece = weights.at[c, pl.ds(pl.multiple_of(x_chip * WIDE, wh), wh)]
        return remote(piece, piece, w2_send.at[c, ny - 1 + o], w2_recv.at[c, ny - 1 + o], device(y_at(o) * 2 + x))

    def w2x(c, o):
        piece = weights.at[c, pl.ds(pl.multiple_of((y_at(ny - o) * 2 + x) * WIDE + wh, wh), wh)]
        return remote(piece, piece, w2_send.at[c, o], w2_recv.at[c, o], device(x_chip))

    def z_copy(c, h, way):
        if way == 0:
            block, to = ch - h, ch + 1
        else:
            block, to = ch + h, ch - 1
        block = jnp.clip(block, 0, n_ch - 1)
        return remote(blocks.at[c, block], blocks.at[c, block], z_send.at[c, h, way], z_recv.at[c, h, way],
                      (ctx, jnp.clip(to, 0, n_ch - 1)))

    def sends(h, way):
        if way == 0:
            return jnp.logical_and(ch >= h, ch < n_ch - 1)
        return jnp.logical_and(ch + h < n_ch, ch > 0)

    def receives(h, way):
        if way == 0:
            return ch - 1 - h >= 0
        return ch + 1 + h < n_ch

    def z_start(c, h):
        for way in range(2):
            @pl.when(sends(h, way))
            def _():
                z_copy(c, h, way).start()

    def z_arrive(c, h):
        for way in range(2):
            @pl.when(receives(h, way))
            def _():
                z_copy(c, h, way).wait_recv()
        if h + 1 < hops:
            z_start(c, h + 1)

    before = remote(prodx.at[pl.ds(tokens, TAPS)], prodx.at[pl.ds(0, TAPS)], halo_sem.at[0], halo_sem.at[1],
                    (jnp.minimum(ctx + 1, n_ctx - 1), ch))
    after = remote(gatex.at[pl.ds(0, TAPS)], gatex.at[pl.ds(tokens, TAPS)], halo_sem.at[2], halo_sem.at[3],
                   (jnp.maximum(ctx - 1, 0), ch))
    gated_copy = remote(gated.at[pl.ds(own, tokens)], gated.at[pl.ds(own, tokens)], pair_sem.at[0], pair_sem.at[1], (other, ch))
    acc_copy = remote(acc.at[pl.ds(theirs, tokens)], acc_in, pair_sem.at[2], pair_sem.at[3], (other, ch))

    def a1(c):
        return remote(a1_out.at[c % 2], a1_in.at[c], a1_send.at[c], a1_recv.at[c], device(x_chip))

    def b1(c, o):
        return remote(b1_out.at[c % 2, o - 1], b1_in.at[c, o - 1], b1_send.at[c, o - 1], b1_recv.at[c, o - 1],
                      device(y_at(o) * 2 + x))

    def a2(c, o):
        return remote(a2_out.at[c % 2, o - 1], a2_in.at[c, o - 1], a2_send.at[c, o - 1], a2_recv.at[c, o - 1],
                      device(y_at(o) * 2 + x))

    def b2(c):
        return remote(b2_out.at[c % 2], b2_in.at[c], b2_send.at[c], b2_recv.at[c], device(x_chip))

    def part(c, target, side):
        return lax.dot_general(
            blocks[c, target], gated[:, side * half : (side + 1) * half], (((0,), (0,)), ((), ())),
            preferred_element_type=F32)

    def phase1(c):
        @pl.when(c >= 2)
        def _():
            a1(c - 2).wait_send()
            for o in range(1, ny):
                b1(c - 2, o).wait_send()

        for ky in range(ny):
            a1_out[c % 2, ky] = part(c, ky * 2 + 1 - x, 0).astype(BF16)
        a1(c).start()
        for o in range(1, ny):
            for kx in range(2):
                b1_out[c % 2, o - 1, kx] = part(c, y_at(o) * 2 + kx, 1).astype(BF16)
            b1(c, o).start()

    def phase2(c):
        @pl.when(c >= 2)
        def _():
            b2(c - 2).wait_send()
            for o in range(1, ny):
                a2(c - 2, o).wait_send()

        a1(c).wait_recv()
        for o in range(1, ny):
            ky = y_at(o)
            a2_out[c % 2, o - 1] = (part(c, ky * 2 + x, 0) + a1_in[c, ky].astype(F32)).astype(BF16)
            a2(c, o).start()
        total = part(c, x_chip, 1)
        for o in range(1, ny):
            b1(c, o).wait_recv()
            total += b1_in[c, o - 1, 1 - x].astype(F32)
        b2_out[c % 2] = total.astype(BF16)
        b2(c).start()

    def phase3(c):
        place = pl.ds(pl.multiple_of(c * WIDE, WIDE), WIDE)
        left = part(c, chip, 0) + a1_in[c, y].astype(F32)
        for o in range(1, ny):
            a2(c, o).wait_recv()
            left += a2_in[c, o - 1].astype(F32)
        g_proj[place, :half] = left
        right = part(c, chip, 1)
        for o in range(1, ny):
            right += b1_in[c, o - 1, x].astype(F32)
        b2(c).wait_recv()
        g_proj[place, half:] = right + b2_in[c].astype(F32)

    def mix_chunk(c):
        for o in range(1, ny):
            w2y(c, o).wait_recv()
            w2x(c, o).wait_recv()

        @pl.loop(0, 2 * tokens // TILE)
        def _(i):
            at = pl.ds(pl.multiple_of(i * TILE, TILE), TILE)
            left = jnp.concatenate([blocks[c, q, at, :] for q in range(n_ch)], 1)
            acc[at, :] += dot32(left, weights[c])

    for load in loads[:2]:
        load.start()
    for c in range(chunks):
        own_copy(c).start()
    for load in loads[2:]:
        load.start()
    for load in w_own:
        load.start()
    pl.semaphore_wait(barrier, n_ctx + 1)

    @pl.loop(0, chunks)
    def _(c):
        swap_copy(c).start()

    @pl.loop(0, chunks)
    def _(c):
        w1x(c).start()
        for o in range(1, ny):
            w1y(c, o).start()

    @pl.loop(0, chunks)
    def _(c):
        own_copy(c).wait()
        swap_copy(c).wait_recv()
        z_start(c, 0)

    for load in loads[:2]:
        load.wait()

    @pl.loop(0, tokens // TAPS)
    def _(i):
        j = tokens // TAPS - 1 - i
        at = pl.ds(pl.multiple_of(j * TAPS, TAPS), TAPS)
        prodx[pl.ds(pl.multiple_of(j * TAPS + TAPS, TAPS), TAPS), :] = (
            key[at, :].astype(F32) * value[at, :].astype(F32)).astype(BF16)

        @pl.when(jnp.logical_and(i == 0, ctx < n_ctx - 1))
        def _():
            before.start()

    @pl.when(ctx == 0)
    def _():
        prodx[:TAPS, :] = jnp.zeros((TAPS, channels), BF16)

    acc[...] = jnp.zeros_like(acc)
    for load in loads[2:]:
        load.wait()

    @pl.when(ctx > 0)
    def _():
        before.wait_recv()

    @pl.loop(0, channels // TILE)
    def _(i):
        at = pl.ds(pl.multiple_of(i * TILE, TILE), TILE)
        f = filt[at, :]
        contract = (((1,), (1,)), ((), ()))
        f_spec = lax.dot_general(thi[:, :TAPS], f, contract, preferred_element_type=F32) + lax.dot_general(
            tlo[:, :TAPS], f, contract, preferred_element_type=F32)
        fspec[:, at] = f_spec
        p_spec = forward(thi[...], tlo[...], prodx[:, at])
        pspec[:, at] = p_spec
        mixed = backward(ihi[TAPS:, :], ilo[TAPS:, :], times(p_spec, f_spec))
        mix[:, at] = mixed
        gated[pl.ds(own, tokens), at] = (query[:, at].astype(F32) * mixed).astype(BF16)

    gated_copy.start()

    for load in w_own:
        load.wait()

    @pl.loop(0, chunks)
    def _(c):
        w1x(c).wait_recv()
        for o in range(1, ny):
            w2y(c, o).start()
        for o in range(1, ny):
            w1y(c, o).wait_recv()
            w2x(c, o).start()
        z_arrive(c, 0)

    gated_copy.wait_recv()

    @pl.loop(0, chunks)
    def _(c):
        for h in range(1, hops):
            z_arrive(c, h)
        phase1(c)

        @pl.when(c >= 1)
        def _():
            phase2(c - 1)

        mix_chunk(c)

        @pl.when(c >= 2)
        def _():
            phase3(c - 2)

    last = chunks - 1
    acc_copy.start()
    phase3(last - 1)
    acc_copy.wait_recv()

    @pl.loop(0, tokens // TAPS)
    def _(i):
        at = pl.ds(pl.multiple_of(i * TAPS, TAPS), TAPS)
        grad_mix = acc[pl.ds(pl.multiple_of(own + i * TAPS, TAPS), TAPS), :] + acc_in[at, :]
        gatex[at, :] = (grad_mix * query[at, :].astype(F32)).astype(BF16)
        g_query[at, :] = (grad_mix * mix[at, :]).astype(BF16)

        @pl.when(jnp.logical_and(i == 0, ctx > 0))
        def _():
            after.start()

    @pl.when(ctx == n_ctx - 1)
    def _():
        gatex[tokens:, :] = jnp.zeros((TAPS, channels), BF16)

    phase2(last)

    share = channels // n_ctx

    def piece(i):
        return pl.ds(pl.multiple_of(i * share, share), share)

    def scatter(off):
        peer = (ctx + off) % n_ctx
        return remote(f_out.at[piece(peer)], f_in.at[off - 1], fs_send.at[off - 1], fs_recv.at[off - 1], (peer, ch))

    def gather(off, source):
        return remote(f_all.at[piece(source)], f_all.at[piece(source)], fg_send.at[off - 1], fg_recv.at[off - 1],
                      ((ctx + off) % n_ctx, ch))

    @pl.loop(0, channels // TILE)
    def _(i):
        at = pl.ds(pl.multiple_of(i * TILE, TILE), TILE)
        own_spec = forward(thi[:, :tokens], tlo[:, :tokens], gatex[:tokens, at])
        taps = backward(lhi[...], llo[...], times_conj(pspec[:, at], own_spec))
        pspec[:, at] = own_spec
        taps = taps.T
        g_filter[at, :] = taps
        f_out[at, :] = taps.astype(BF16)

    @pl.loop(1, n_ctx)
    def _(off):
        scatter(off).start()

    @pl.when(ctx < n_ctx - 1)
    def _():
        after.wait_recv()

    @pl.loop(0, channels // TILE)
    def _(i):
        at = pl.ds(pl.multiple_of(i * TILE, TILE), TILE)
        gate_spec = pspec[:, at] + forward(thi[:, tokens:], tlo[:, tokens:], gatex[tokens:, at])
        grad_prod = backward(ihi[:tokens, :], ilo[:tokens, :], times_conj(gate_spec, fspec[:, at]))
        g_key[:, at] = (grad_prod * value[:, at].astype(F32)).astype(BF16)
        g_value[:, at] = (grad_prod * key[:, at].astype(F32)).astype(BF16)

    total = g_filter[piece(ctx), :]
    for off in range(1, n_ctx):
        scatter(off).wait_recv()
        total += f_in[off - 1].astype(F32)
    f_all[piece(ctx), :] = total.astype(BF16)

    @pl.loop(1, n_ctx)
    def _(off):
        gather(off, ctx).start()

    phase3(last)

    @pl.loop(1, n_ctx)
    def _(off):
        gather(off, (ctx + n_ctx - off) % n_ctx).wait_recv()

    g_filter[...] = f_all[...].astype(F32)

    @pl.loop(1, n_ctx)
    def _(off):
        gather(off, ctx).wait_send()
        scatter(off).wait_send()

    @pl.when(ctx < n_ctx - 1)
    def _():
        before.wait_send()

    @pl.when(ctx > 0)
    def _():
        after.wait_send()

    gated_copy.wait_send()
    acc_copy.wait_send()

    @pl.loop(0, chunks)
    def _(c):
        swap_copy(c).wait_send()
        w1x(c).wait_send()
        for o in range(1, ny):
            w1y(c, o).wait_send()
            w2y(c, o).wait_send()
            w2x(c, o).wait_send()
        for h in range(hops):
            for way in range(2):
                @pl.when(sends(h, way))
                def _():
                    z_copy(c, h, way).wait_send()

    for c in (last - 1, last):
        a1(c).wait_send()
        b2(c).wait_send()
        for o in range(1, ny):
            b1(c, o).wait_send()
            a2(c, o).wait_send()


def shards(query_act, key_act, value_act, filters, proj_weight, cotangent):
    n_ctx, n_ch = lax.axis_size("ctx"), lax.axis_size("ch")
    tokens, channels = query_act.shape
    rows = proj_weight.shape[0]
    assert n_ctx == 2 * n_ch and cotangent.shape[1] == 2 * rows
    chunks, ny, hops = rows // WIDE, n_ctx // 4, n_ch - 1
    points = tokens + TAPS
    half, share = channels // 2, channels // n_ctx
    table = basis(points)
    inverse = (table.T / (points // 2)).astype(np.float32)
    lags = inverse[TAPS - np.arange(TAPS)]
    tables = [jnp.asarray(t) for pair in (table, inverse, lags) for t in constant_pair(pair)]
    dma = pltpu.SemaphoreType.DMA
    vmem = pltpu.VMEM
    outs = pl.pallas_call(
        functools.partial(kernel, n_ctx, n_ch),
        out_shape=(
            jax.ShapeDtypeStruct((tokens, channels), BF16),
            jax.ShapeDtypeStruct((tokens, channels), BF16),
            jax.ShapeDtypeStruct((tokens, channels), BF16),
            jax.ShapeDtypeStruct((channels, TAPS), F32),
            jax.ShapeDtypeStruct((rows, channels), F32),
        ),
        in_specs=[pl.BlockSpec(memory_space=pl.ANY)] * 12,
        out_specs=[pl.BlockSpec(memory_space=pltpu.VMEM)] * 5,
        scratch_shapes=[
            vmem((chunks, n_ch, 2 * tokens, WIDE), BF16),
            vmem((chunks, n_ch * WIDE, channels), BF16),
            vmem((2 * tokens, channels), F32),
            vmem((tokens, channels), F32),
            vmem((tokens, channels), BF16),
            vmem((tokens, channels), BF16),
            vmem((tokens, channels), BF16),
            vmem((channels, TAPS), BF16),
            vmem((points, points), BF16),
            vmem((points, points), BF16),
            vmem((points, points), BF16),
            vmem((points, points), BF16),
            vmem((TAPS, points), BF16),
            vmem((TAPS, points), BF16),
            vmem((points, channels), BF16),
            vmem((points, channels), BF16),
            vmem((2 * tokens, channels), BF16),
            vmem((tokens, channels), F32),
            vmem((points, channels), F32),
            vmem((points, channels), F32),
            vmem((2, ny, WIDE, half), BF16),
            vmem((2, ny - 1, 2, WIDE, half), BF16),
            vmem((2, ny - 1, WIDE, half), BF16),
            vmem((2, WIDE, half), BF16),
            vmem((chunks, ny, WIDE, half), BF16),
            vmem((chunks, ny - 1, 2, WIDE, half), BF16),
            vmem((chunks, ny - 1, WIDE, half), BF16),
            vmem((chunks, WIDE, half), BF16),
            vmem((channels, TAPS), BF16),
            vmem((n_ctx - 1, share, TAPS), BF16),
            vmem((channels, TAPS), BF16),
            dma((10 + chunks,)),
            dma((chunks,)),
            dma((2, chunks)),
            dma((chunks, hops, 2)),
            dma((chunks, hops, 2)),
            dma((chunks, ny)),
            dma((chunks, ny)),
            dma((chunks, 2 * ny)),
            dma((chunks, 2 * ny)),
            dma((chunks,)),
            dma((chunks,)),
            dma((chunks, ny - 1)),
            dma((chunks, ny - 1)),
            dma((chunks, ny - 1)),
            dma((chunks, ny - 1)),
            dma((chunks,)),
            dma((chunks,)),
            dma((4,)),
            dma((4,)),
            dma((n_ctx - 1,)),
            dma((n_ctx - 1,)),
            dma((n_ctx - 1,)),
            dma((n_ctx - 1,)),
        ],
        compiler_params=pltpu.CompilerParams(
            collective_id=0, has_side_effects=True, vmem_limit_bytes=63 * 2**20
        ),
    )(query_act, key_act, value_act, filters, proj_weight, cotangent, *tables)
    return tuple(outs)


def solution(mesh):
    return jax.shard_map(
        shards,
        mesh=mesh,
        in_specs=(
            P("ctx", "ch"),
            P("ctx", "ch"),
            P("ctx", "ch"),
            P("ch", None),
            P("ctx", "ch"),
            P("ctx", "ch"),
        ),
        out_specs=(P("ctx", "ch"), P("ctx", "ch"), P("ctx", "ch"), P("ch", None), P("ctx", "ch")),
        check_vma=False,
    )
```

```python
import functools

import jax
import jax.numpy as jnp
import ml_dtypes
import numpy as np
from jax import lax
from jax.experimental import pallas as pl
from jax.experimental.pallas import tpu as pltpu
from jax.sharding import PartitionSpec as P

TAPS = 128
WIDE = 128
TILE = 256
AHEAD = 3
MESH = pl.DeviceIdType.MESH
BF16 = jnp.bfloat16
F32 = jnp.float32


def basis(points):
    freqs = points // 2
    phase = (2 * np.arange(freqs)[:, None] + 1) * np.arange(points)[None, :] % (2 * points)
    angle = np.pi * phase / points
    return np.concatenate([np.cos(angle), np.sin(angle)], 0).astype(np.float32)


def constant_pair(a):
    hi = a.astype(ml_dtypes.bfloat16)
    lo = (a - hi.astype(np.float32)).astype(ml_dtypes.bfloat16)
    return hi, lo


def split(a):
    hi = a.astype(BF16)
    return hi, (a - hi.astype(F32)).astype(BF16)


def dot32(a, b):
    return jnp.dot(a, b, preferred_element_type=F32)


def forward(hi, lo, x):
    return dot32(hi, x) + dot32(lo, x)


def backward(thi, tlo, y):
    yhi, ylo = split(y)
    return dot32(thi, yhi) + dot32(thi, ylo) + dot32(tlo, yhi)


def halves(x):
    n = x.shape[0] // 2
    return x[:n], x[n:]


def times(x, f):
    (xc, xs), (fc, fs) = halves(x), halves(f)
    return jnp.concatenate([xc * fc - xs * fs, xc * fs + xs * fc], 0)


def times_conj(x, f):
    (xc, xs), (fc, fs) = halves(x), halves(f)
    return jnp.concatenate([xc * fc + xs * fs, xs * fc - xc * fs], 0)


def kernel(n_ctx, n_ch, query_in, key_in, value_in, filt_in, weight, cot, thi_in, tlo_in, ihi_in, ilo_in, lhi_in, llo_in,
           g_query, g_key, g_value, g_filter, g_proj,
           blocks, weights, acc, acc_in, query, key, value, filt, thi, tlo, ihi, ilo, lhi, llo,
           prodx, gatex, gated, mix, pspec, fspec,
           a1_out, b1_out, a2_out, b2_out, a1_in, b1_in, a2_in, b2_in, f_out, f_in, f_all,
           s_query, s_key, s_value, s_filter, s_proj, store_sem, proj_sem,
           load_sem, own_sem, swap_sem, z_send, z_recv, w1_send, w1_recv, w2_send, w2_recv,
           a1_send, a1_recv, b1_send, b1_recv, a2_send, a2_recv, b2_send, b2_recv,
           halo_sem, pair_sem, fs_send, fs_recv, fg_send, fg_recv):
    chips = n_ctx // 2
    ny = chips // 2
    hops = n_ch - 1
    ctx = lax.axis_index("ctx")
    ch = lax.axis_index("ch")
    chip, core = ctx // 2, ctx % 2
    y, x = chip // 2, chip % 2
    other = chip * 2 + 1 - core
    x_chip = y * 2 + 1 - x
    tokens = query.shape[0]
    channels = query.shape[1]
    rows = weight.shape[0]
    chunks = rows // WIDE
    half = channels // 2
    wh = WIDE // 2
    own = pl.multiple_of(core * tokens, tokens)
    theirs = pl.multiple_of((1 - core) * tokens, tokens)

    def device(c):
        return (c * 2 + core, ch)

    def y_at(o):
        return (y + o) % ny

    def remote(src, dst, send, recv, to):
        return pltpu.make_async_remote_copy(src, dst, send, recv, device_id=to, device_id_type=MESH)

    barrier = pltpu.get_barrier_semaphore()
    for off in range(1, n_ctx):
        pl.semaphore_signal(barrier, inc=1, device_id=((ctx + off) % n_ctx, ch), device_id_type=MESH)
    for off in (1, n_ch - 1):
        pl.semaphore_signal(barrier, inc=1, device_id=(ctx, (ch + off) % n_ch), device_id_type=MESH)

    loads = [pltpu.make_async_copy(a, b, load_sem.at[i]) for i, (a, b) in enumerate((
        (key_in, key), (value_in, value), (filt_in, filt), (thi_in, thi), (tlo_in, tlo), (ihi_in, ihi), (ilo_in, ilo),
        (query_in, query), (lhi_in, lhi), (llo_in, llo)))]

    def own_copy(c):
        return pltpu.make_async_copy(
            cot.at[:, pl.ds(pl.multiple_of(core * rows + c * WIDE, WIDE), WIDE)],
            blocks.at[c, ch, pl.ds(own, tokens)], own_sem.at[c])

    def swap_copy(c):
        return remote(
            cot.at[:, pl.ds(pl.multiple_of((1 - core) * rows + c * WIDE, WIDE), WIDE)],
            blocks.at[c, ch, pl.ds(own, tokens)], swap_sem.at[0, c], swap_sem.at[1, c], (other, ch))

    def w_rows(c, q):
        return weights.at[c, pl.ds(pl.multiple_of(q * WIDE, WIDE), WIDE)]

    def w_piece(c):
        return weight.at[pl.ds(pl.multiple_of(c * WIDE, WIDE), WIDE)]

    w_own = [pltpu.make_async_copy(w_piece(c), w_rows(c, chip), load_sem.at[len(loads) + c]) for c in range(chunks)]

    def w1x(c):
        return remote(w_piece(c), w_rows(c, chip), w1_send.at[c, 0], w1_recv.at[c, 0], device(x_chip))

    def w1y(c, o):
        return remote(w_piece(c), w_rows(c, chip), w1_send.at[c, o], w1_recv.at[c, o], device(y_at(o) * 2 + x))

    def w2y(c, o):
        piece = weights.at[c, pl.ds(pl.multiple_of(x_chip * WIDE, wh), wh)]
        return remote(piece, piece, w2_send.at[c, ny - 1 + o], w2_recv.at[c, ny - 1 + o], device(y_at(o) * 2 + x))

    def w2x(c, o):
        piece = weights.at[c, pl.ds(pl.multiple_of((y_at(ny - o) * 2 + x) * WIDE + wh, wh), wh)]
        return remote(piece, piece, w2_send.at[c, o], w2_recv.at[c, o], device(x_chip))

    def z_copy(c, h, way):
        if way == 0:
            block, to = ch - h, ch + 1
        else:
            block, to = ch + h, ch - 1
        block = jnp.clip(block, 0, n_ch - 1)
        return remote(blocks.at[c, block], blocks.at[c, block], z_send.at[c, h, way], z_recv.at[c, h, way],
                      (ctx, jnp.clip(to, 0, n_ch - 1)))

    def sends(h, way):
        if way == 0:
            return jnp.logical_and(ch >= h, ch < n_ch - 1)
        return jnp.logical_and(ch + h < n_ch, ch > 0)

    def receives(h, way):
        if way == 0:
            return ch - 1 - h >= 0
        return ch + 1 + h < n_ch

    def z_start(c, h):
        for way in range(2):
            @pl.when(sends(h, way))
            def _():
                z_copy(c, h, way).start()

    def z_arrive(c, h):
        for way in range(2):
            @pl.when(receives(h, way))
            def _():
                z_copy(c, h, way).wait_recv()
        if h + 1 < hops:
            z_start(c, h + 1)

    before = remote(prodx.at[pl.ds(tokens, TAPS)], prodx.at[pl.ds(0, TAPS)], halo_sem.at[0], halo_sem.at[1],
                    (jnp.minimum(ctx + 1, n_ctx - 1), ch))
    after = remote(gatex.at[pl.ds(0, TAPS)], gatex.at[pl.ds(tokens, TAPS)], halo_sem.at[2], halo_sem.at[3],
                   (jnp.maximum(ctx - 1, 0), ch))
    gated_copy = remote(gated.at[pl.ds(own, tokens)], gated.at[pl.ds(own, tokens)], pair_sem.at[0, 0], pair_sem.at[1, 0],
                        (other, ch))

    def acc_copy(t):
        there = pl.ds(pl.multiple_of(theirs + t * TILE, TILE), TILE)
        return remote(acc.at[there], acc_in.at[pl.ds(pl.multiple_of(t * TILE, TILE), TILE)],
                      pair_sem.at[2, t], pair_sem.at[3, t], (other, ch))

    def columns(t):
        return pl.ds(pl.multiple_of(t * TILE, TILE), TILE)

    def key_store(t):
        return pltpu.make_async_copy(s_key.at[:, columns(t)], g_key.at[:, columns(t)], store_sem.at[0, t])

    def value_store(t):
        return pltpu.make_async_copy(s_value.at[:, columns(t)], g_value.at[:, columns(t)], store_sem.at[1, t])

    def query_store(t):
        at = pl.ds(pl.multiple_of(t * TAPS, TAPS), TAPS)
        return pltpu.make_async_copy(s_query.at[at], g_query.at[at], store_sem.at[2, t])

    def proj_store(c):
        place = pl.ds(pl.multiple_of(c * WIDE, WIDE), WIDE)
        return pltpu.make_async_copy(s_proj.at[c % 2], g_proj.at[place], proj_sem.at[c])

    filter_store = pltpu.make_async_copy(s_filter, g_filter, store_sem.at[3, 0])

    def a1(c):
        return remote(a1_out.at[c % 2], a1_in.at[c], a1_send.at[c], a1_recv.at[c], device(x_chip))

    def b1(c, o):
        return remote(b1_out.at[c % 2, o - 1], b1_in.at[c, o - 1], b1_send.at[c, o - 1], b1_recv.at[c, o - 1],
                      device(y_at(o) * 2 + x))

    def a2(c, o):
        return remote(a2_out.at[c % 2, o - 1], a2_in.at[c, o - 1], a2_send.at[c, o - 1], a2_recv.at[c, o - 1],
                      device(y_at(o) * 2 + x))

    def b2(c):
        return remote(b2_out.at[c % 2], b2_in.at[c], b2_send.at[c], b2_recv.at[c], device(x_chip))

    def part(c, target, side):
        return lax.dot_general(
            blocks[c, target], gated[:, side * half : (side + 1) * half], (((0,), (0,)), ((), ())),
            preferred_element_type=F32)

    def phase1(c):
        @pl.when(c >= 2)
        def _():
            a1(c - 2).wait_send()
            for o in range(1, ny):
                b1(c - 2, o).wait_send()

        for ky in range(ny):
            a1_out[c % 2, ky] = part(c, ky * 2 + 1 - x, 0).astype(BF16)
        a1(c).start()
        for o in range(1, ny):
            for kx in range(2):
                b1_out[c % 2, o - 1, kx] = part(c, y_at(o) * 2 + kx, 1).astype(BF16)
            b1(c, o).start()

    def phase2(c):
        @pl.when(c >= 2)
        def _():
            b2(c - 2).wait_send()
            for o in range(1, ny):
                a2(c - 2, o).wait_send()

        a1(c).wait_recv()
        for o in range(1, ny):
            ky = y_at(o)
            a2_out[c % 2, o - 1] = (part(c, ky * 2 + x, 0) + a1_in[c, ky].astype(F32)).astype(BF16)
            a2(c, o).start()
        total = part(c, x_chip, 1)
        for o in range(1, ny):
            b1(c, o).wait_recv()
            total += b1_in[c, o - 1, 1 - x].astype(F32)
        b2_out[c % 2] = total.astype(BF16)
        b2(c).start()

    def phase3(c):
        @pl.when(c >= 2)
        def _():
            proj_store(c - 2).wait()

        left = part(c, chip, 0) + a1_in[c, y].astype(F32)
        for o in range(1, ny):
            a2(c, o).wait_recv()
            left += a2_in[c, o - 1].astype(F32)
        s_proj[c % 2, :, :half] = left
        right = part(c, chip, 1)
        for o in range(1, ny):
            right += b1_in[c, o - 1, x].astype(F32)
        b2(c).wait_recv()
        s_proj[c % 2, :, half:] = right + b2_in[c].astype(F32)
        proj_store(c).start()

    def mix_chunk(c):
        for o in range(1, ny):
            w2y(c, o).wait_recv()
            w2x(c, o).wait_recv()

        for first in (theirs, own):
            @pl.loop(0, tokens // TILE)
            def _(i):
                at = pl.ds(pl.multiple_of(first + i * TILE, TILE), TILE)
                left = jnp.concatenate([blocks[c, q, at, :] for q in range(n_ch)], 1)
                acc[at, :] += dot32(left, weights[c])
                if first is theirs:
                    @pl.when(c == chunks - 1)
                    def _():
                        acc_copy(i).start()

    for load in loads[:2]:
        load.start()
    for c in range(chunks):
        own_copy(c).start()
    for load in loads[2:]:
        load.start()
    for load in w_own:
        load.start()
    pl.semaphore_wait(barrier, n_ctx + 1)

    @pl.loop(0, chunks)
    def _(c):
        swap_copy(c).start()

    def w_start(c):
        w1x(c).start()
        for o in range(1, ny):
            w1y(c, o).start()

    def w_arrive(c):
        w1x(c).wait_recv()
        for o in range(1, ny):
            w2y(c, o).start()
        for o in range(1, ny):
            w1y(c, o).wait_recv()
            w2x(c, o).start()

    def product(j):
        at = pl.ds(pl.multiple_of(j * TAPS, TAPS), TAPS)
        prodx[pl.ds(pl.multiple_of(j * TAPS + TAPS, TAPS), TAPS), :] = (
            key[at, :].astype(F32) * value[at, :].astype(F32)).astype(BF16)

    for load in loads[:2]:
        load.wait()
    product(tokens // TAPS - 1)

    @pl.when(ctx < n_ctx - 1)
    def _():
        before.start()

    @pl.loop(0, min(4, chunks))
    def _(c):
        w_start(c)

    @pl.loop(0, chunks)
    def _(c):
        own_copy(c).wait()
        swap_copy(c).wait_recv()

        @pl.when(c < AHEAD)
        def _():
            z_start(c, 0)

    pl.loop(0, tokens // TAPS - 1)(product)

    @pl.when(ctx == 0)
    def _():
        prodx[:TAPS, :] = jnp.zeros((TAPS, channels), BF16)

    acc[...] = jnp.zeros_like(acc)
    for load in loads[2:]:
        load.wait()

    @pl.when(ctx > 0)
    def _():
        before.wait_recv()

    @pl.loop(0, channels // TILE)
    def _(i):
        at = pl.ds(pl.multiple_of(i * TILE, TILE), TILE)
        f = filt[at, :]
        contract = (((1,), (1,)), ((), ()))
        f_spec = lax.dot_general(thi[:, :TAPS], f, contract, preferred_element_type=F32) + lax.dot_general(
            tlo[:, :TAPS], f, contract, preferred_element_type=F32)
        fspec[:, at] = f_spec
        p_spec = forward(thi[...], tlo[...], prodx[:, at])
        pspec[:, at] = p_spec
        mixed = backward(ihi[TAPS:, :], ilo[TAPS:, :], times(p_spec, f_spec))
        mix[:, at] = mixed
        gated[pl.ds(own, tokens), at] = (query[:, at].astype(F32) * mixed).astype(BF16)

    gated_copy.start()

    for load in w_own:
        load.wait()

    @pl.loop(0, min(2, chunks))
    def _(c):
        w_arrive(c)

    gated_copy.wait_recv()
    close = max(chunks - 3, 1)

    def sent(c):
        return jnp.where(c < close, jnp.maximum(c - 1, 0), c)

    def mixed_up_to(c):
        return jnp.where(c < close, c, c + 1)

    @pl.loop(0, chunks)
    def _(c):
        z_arrive(c, 0)

        @pl.when(c + 2 < chunks)
        def _():
            w_arrive(c + 2)

        @pl.when(c + 4 < chunks)
        def _():
            w_start(c + 4)

        for h in range(1, hops - 1):
            z_arrive(c, h)

        @pl.when(jnp.logical_and(c + 1 >= AHEAD, c + 1 < chunks))
        def _():
            z_start(c + 1, 0)

        pl.loop(sent(c - 1), sent(c))(phase2)
        pl.loop(sent(c - 2), sent(c - 1))(phase3)
        z_arrive(c, hops - 1)
        phase1(c)
        pl.loop(jnp.maximum(mixed_up_to(c - 1), 0), mixed_up_to(c))(mix_chunk)

    last = chunks - 1

    @pl.loop(0, tokens // TAPS)
    def _(i):
        @pl.when(i % (TILE // TAPS) == 0)
        def _():
            acc_copy(i // (TILE // TAPS)).wait_recv()

        at = pl.ds(pl.multiple_of(i * TAPS, TAPS), TAPS)
        grad_mix = acc[pl.ds(pl.multiple_of(own + i * TAPS, TAPS), TAPS), :] + acc_in[at, :]
        gatex[at, :] = (grad_mix * query[at, :].astype(F32)).astype(BF16)

        @pl.when(jnp.logical_and(i == 0, ctx > 0))
        def _():
            after.start()

        s_query[at, :] = (grad_mix * mix[at, :]).astype(BF16)
        query_store(i).start()

    @pl.when(ctx == n_ctx - 1)
    def _():
        gatex[tokens:, :] = jnp.zeros((TAPS, channels), BF16)

    share = channels // n_ctx

    def piece(i):
        return pl.ds(pl.multiple_of(i * share, share), share)

    def scatter(off):
        peer = (ctx + off) % n_ctx
        return remote(f_out.at[piece(peer)], f_in.at[off - 1], fs_send.at[off - 1], fs_recv.at[off - 1], (peer, ch))

    def gather(off, source):
        return remote(f_all.at[piece(source)], f_all.at[piece(source)], fg_send.at[off - 1], fg_recv.at[off - 1],
                      ((ctx + off) % n_ctx, ch))

    @pl.loop(0, channels // TILE)
    def _(i):
        at = pl.ds(pl.multiple_of(i * TILE, TILE), TILE)
        own_spec = forward(thi[:, :tokens], tlo[:, :tokens], gatex[:tokens, at])
        taps = backward(lhi[...], llo[...], times_conj(pspec[:, at], own_spec))
        pspec[:, at] = own_spec
        taps = taps.T
        s_filter[at, :] = taps
        f_out[at, :] = taps.astype(BF16)

    @pl.loop(1, n_ctx)
    def _(off):
        scatter(off).start()

    phase2(last)
    phase3(last - 1)

    @pl.when(ctx < n_ctx - 1)
    def _():
        after.wait_recv()

    @pl.loop(0, channels // TILE)
    def _(i):
        at = pl.ds(pl.multiple_of(i * TILE, TILE), TILE)
        gate_spec = pspec[:, at] + forward(thi[:, tokens:], tlo[:, tokens:], gatex[tokens:, at])
        grad_prod = backward(ihi[:tokens, :], ilo[:tokens, :], times_conj(gate_spec, fspec[:, at]))
        s_key[:, at] = (grad_prod * value[:, at].astype(F32)).astype(BF16)
        s_value[:, at] = (grad_prod * key[:, at].astype(F32)).astype(BF16)
        key_store(i).start()
        value_store(i).start()

    total = s_filter[piece(ctx), :]
    for off in range(1, n_ctx):
        scatter(off).wait_recv()
        total += f_in[off - 1].astype(F32)
    f_all[piece(ctx), :] = total.astype(BF16)

    @pl.loop(1, n_ctx)
    def _(off):
        gather(off, ctx).start()

    phase3(last)

    @pl.loop(1, n_ctx)
    def _(off):
        gather(off, (ctx + n_ctx - off) % n_ctx).wait_recv()

    s_filter[...] = f_all[...].astype(F32)
    filter_store.start()

    @pl.loop(1, n_ctx)
    def _(off):
        gather(off, ctx).wait_send()
        scatter(off).wait_send()

    @pl.when(ctx < n_ctx - 1)
    def _():
        before.wait_send()

    @pl.when(ctx > 0)
    def _():
        after.wait_send()

    gated_copy.wait_send()
    filter_store.wait()

    @pl.loop(0, tokens // TILE)
    def _(i):
        acc_copy(i).wait_send()

    @pl.loop(0, tokens // TAPS)
    def _(i):
        query_store(i).wait()

    @pl.loop(0, channels // TILE)
    def _(i):
        key_store(i).wait()
        value_store(i).wait()

    for c in (last - 1, last):
        proj_store(c).wait()

    @pl.loop(0, chunks)
    def _(c):
        swap_copy(c).wait_send()
        w1x(c).wait_send()
        for o in range(1, ny):
            w1y(c, o).wait_send()
            w2y(c, o).wait_send()
            w2x(c, o).wait_send()
        for h in range(hops):
            for way in range(2):
                @pl.when(sends(h, way))
                def _():
                    z_copy(c, h, way).wait_send()

    for c in (last - 1, last):
        a1(c).wait_send()
        b2(c).wait_send()
        for o in range(1, ny):
            b1(c, o).wait_send()
            a2(c, o).wait_send()


PIECES = 4


def hand_over_kernel(n, *refs):
    ins, outs, held = refs[:n], refs[n : 2 * n], refs[2 * n : 3 * n]
    in_sem, out_sem = refs[3 * n :]
    steps = []
    for i in range(n):
        size = ins[i].shape[0] // PIECES
        for p in range(PIECES):
            at = pl.ds(p * size, size)
            steps.append((pltpu.make_async_copy(ins[i].at[at], held[i].at[at], in_sem.at[i, p]),
                          pltpu.make_async_copy(held[i].at[at], outs[i].at[at], out_sem.at[i, p])))
    for read, _ in steps:
        read.start()
    for read, write in steps:
        read.wait()
        write.start()
    for _, write in steps:
        write.wait()


def hand_over(arrays):
    n = len(arrays)
    return tuple(pl.pallas_call(
        functools.partial(hand_over_kernel, n),
        out_shape=tuple(jax.ShapeDtypeStruct(a.shape, a.dtype) for a in arrays),
        in_specs=[pl.BlockSpec(memory_space=pl.ANY)] * n,
        out_specs=[pl.BlockSpec(memory_space=pl.ANY)] * n,
        scratch_shapes=[pltpu.VMEM(a.shape, a.dtype) for a in arrays]
        + [pltpu.SemaphoreType.DMA((n, PIECES))] * 2,
        compiler_params=pltpu.CompilerParams(vmem_limit_bytes=62 * 2**20),
    )(*arrays))


def shards(query_act, key_act, value_act, filters, proj_weight, cotangent):
    n_ctx, n_ch = lax.axis_size("ctx"), lax.axis_size("ch")
    tokens, channels = query_act.shape
    rows = proj_weight.shape[0]
    assert n_ctx == 2 * n_ch and cotangent.shape[1] == 2 * rows
    chunks, ny, hops = rows // WIDE, n_ctx // 4, n_ch - 1
    points = tokens + TAPS
    half, share = channels // 2, channels // n_ctx
    table = basis(points)
    inverse = (table.T / (points // 2)).astype(np.float32)
    lags = inverse[TAPS - np.arange(TAPS)]
    tables = [jnp.asarray(t) for pair in (table, inverse, lags) for t in constant_pair(pair)]
    dma = pltpu.SemaphoreType.DMA
    vmem = pltpu.VMEM
    outs = pl.pallas_call(
        functools.partial(kernel, n_ctx, n_ch),
        out_shape=(
            jax.ShapeDtypeStruct((tokens, channels), BF16),
            jax.ShapeDtypeStruct((tokens, channels), BF16),
            jax.ShapeDtypeStruct((tokens, channels), BF16),
            jax.ShapeDtypeStruct((channels, TAPS), F32),
            jax.ShapeDtypeStruct((rows, channels), F32),
        ),
        in_specs=[pl.BlockSpec(memory_space=pl.ANY)] * 12,
        out_specs=[pl.BlockSpec(memory_space=pl.ANY)] * 5,
        scratch_shapes=[
            vmem((chunks, n_ch, 2 * tokens, WIDE), BF16),
            vmem((chunks, n_ch * WIDE, channels), BF16),
            vmem((2 * tokens, channels), F32),
            vmem((tokens, channels), F32),
            vmem((tokens, channels), BF16),
            vmem((tokens, channels), BF16),
            vmem((tokens, channels), BF16),
            vmem((channels, TAPS), BF16),
            vmem((points, points), BF16),
            vmem((points, points), BF16),
            vmem((points, points), BF16),
            vmem((points, points), BF16),
            vmem((TAPS, points), BF16),
            vmem((TAPS, points), BF16),
            vmem((points, channels), BF16),
            vmem((points, channels), BF16),
            vmem((2 * tokens, channels), BF16),
            vmem((tokens, channels), F32),
            vmem((points, channels), F32),
            vmem((points, channels), F32),
            vmem((2, ny, WIDE, half), BF16),
            vmem((2, ny - 1, 2, WIDE, half), BF16),
            vmem((2, ny - 1, WIDE, half), BF16),
            vmem((2, WIDE, half), BF16),
            vmem((chunks, ny, WIDE, half), BF16),
            vmem((chunks, ny - 1, 2, WIDE, half), BF16),
            vmem((chunks, ny - 1, WIDE, half), BF16),
            vmem((chunks, WIDE, half), BF16),
            vmem((channels, TAPS), BF16),
            vmem((n_ctx - 1, share, TAPS), BF16),
            vmem((channels, TAPS), BF16),
            vmem((tokens, channels), BF16),
            vmem((tokens, channels), BF16),
            vmem((tokens, channels), BF16),
            vmem((channels, TAPS), F32),
            vmem((2, WIDE, channels), F32),
            dma((4, max(channels // TILE, tokens // TAPS))),
            dma((chunks,)),
            dma((10 + chunks,)),
            dma((chunks,)),
            dma((2, chunks)),
            dma((chunks, hops, 2)),
            dma((chunks, hops, 2)),
            dma((chunks, ny)),
            dma((chunks, ny)),
            dma((chunks, 2 * ny)),
            dma((chunks, 2 * ny)),
            dma((chunks,)),
            dma((chunks,)),
            dma((chunks, ny - 1)),
            dma((chunks, ny - 1)),
            dma((chunks, ny - 1)),
            dma((chunks, ny - 1)),
            dma((chunks,)),
            dma((chunks,)),
            dma((4,)),
            dma((4, tokens // TILE)),
            dma((n_ctx - 1,)),
            dma((n_ctx - 1,)),
            dma((n_ctx - 1,)),
            dma((n_ctx - 1,)),
        ],
        compiler_params=pltpu.CompilerParams(
            collective_id=0, has_side_effects=True, vmem_limit_bytes=63 * 2**20
        ),
    )(query_act, key_act, value_act, filters, proj_weight, cotangent, *tables)
    return hand_over(outs)


def solution(mesh):
    return jax.shard_map(
        shards,
        mesh=mesh,
        in_specs=(
            P("ctx", "ch"),
            P("ctx", "ch"),
            P("ctx", "ch"),
            P("ch", None),
            P("ctx", "ch"),
            P("ctx", "ch"),
        ),
        out_specs=(P("ctx", "ch"), P("ctx", "ch"), P("ctx", "ch"), P("ch", None), P("ctx", "ch")),
        check_vma=False,
    )
```

```python
import functools

import jax
import jax.numpy as jnp
import ml_dtypes
import numpy as np
from jax import lax
from jax.experimental import pallas as pl
from jax.experimental.pallas import tpu as pltpu
from jax.sharding import PartitionSpec as P

TAPS = 128
WIDE = 128
TILE = 256
COLUMNS = 512
AHEAD = 3
MESH = pl.DeviceIdType.MESH
BF16 = jnp.bfloat16
F32 = jnp.float32


def basis(points):
    freqs = points // 2
    phase = (2 * np.arange(freqs)[:, None] + 1) * np.arange(points)[None, :] % (2 * points)
    angle = np.pi * phase / points
    return np.concatenate([np.cos(angle), np.sin(angle)], 0).astype(np.float32)


def constant_pair(a):
    hi = a.astype(ml_dtypes.bfloat16)
    lo = (a - hi.astype(np.float32)).astype(ml_dtypes.bfloat16)
    return hi, lo


def split(a):
    hi = a.astype(BF16)
    return hi, (a - hi.astype(F32)).astype(BF16)


def dot32(a, b):
    return jnp.dot(a, b, preferred_element_type=F32)


def pair_columns(a):
    hi, lo = constant_pair(a)
    blocks = [t[:, i : i + TAPS] for i in range(0, a.shape[1], TAPS) for t in (hi, lo)]
    return np.concatenate(blocks, 1)


def triple_columns(a):
    hi, lo = constant_pair(a)
    return np.concatenate([hi, hi, lo], 1)


def forward(table, x):
    blocks = [x[i : i + TAPS] for i in range(0, x.shape[0], TAPS) for _ in range(2)]
    return dot32(table, jnp.concatenate(blocks, 0))


def backward(table, y):
    hi, lo = split(y)
    return dot32(table, jnp.concatenate([hi, lo, hi], 0))


def halves(x):
    n = x.shape[0] // 2
    return x[:n], x[n:]


def times(x, f):
    (xc, xs), (fc, fs) = halves(x), halves(f)
    return jnp.concatenate([xc * fc - xs * fs, xc * fs + xs * fc], 0)


def times_conj(x, f):
    (xc, xs), (fc, fs) = halves(x), halves(f)
    return jnp.concatenate([xc * fc + xs * fs, xs * fc - xc * fs], 0)


def kernel(n_ctx, n_ch, query_in, key_in, value_in, filt_in, weight, cot, table_in, inverse_in, lags_in,
           g_query, g_key, g_value, g_filter, g_proj,
           blocks, weights, acc, acc_in, query, key, value, filt, table, inverse, lags,
           prodx, gatex, gated, mix, pspec, fspec,
           a1_out, b1_out, a2_out, b2_out, a1_in, b1_in, a2_in, b2_in, f_out, f_in, f_all,
           s_query, s_key, s_value, s_filter, s_proj, store_sem, proj_sem,
           load_sem, own_sem, swap_sem, z_send, z_recv, w1_send, w1_recv, w2_send, w2_recv,
           a1_send, a1_recv, b1_send, b1_recv, a2_send, a2_recv, b2_send, b2_recv,
           halo_sem, pair_sem, fs_send, fs_recv, fg_send, fg_recv):
    chips = n_ctx // 2
    ny = chips // 2
    hops = n_ch - 1
    ctx = lax.axis_index("ctx")
    ch = lax.axis_index("ch")
    chip, core = ctx // 2, ctx % 2
    y, x = chip // 2, chip % 2
    other = chip * 2 + 1 - core
    x_chip = y * 2 + 1 - x
    tokens = query.shape[0]
    channels = query.shape[1]
    rows = weight.shape[0]
    chunks = rows // WIDE
    half = channels // 2
    wh = WIDE // 2
    own = pl.multiple_of(core * tokens, tokens)
    theirs = pl.multiple_of((1 - core) * tokens, tokens)

    def device(c):
        return (c * 2 + core, ch)

    def y_at(o):
        return (y + o) % ny

    def remote(src, dst, send, recv, to):
        return pltpu.make_async_remote_copy(src, dst, send, recv, device_id=to, device_id_type=MESH)

    barrier = pltpu.get_barrier_semaphore()
    for off in range(1, n_ctx):
        pl.semaphore_signal(barrier, inc=1, device_id=((ctx + off) % n_ctx, ch), device_id_type=MESH)
    for off in (1, n_ch - 1):
        pl.semaphore_signal(barrier, inc=1, device_id=(ctx, (ch + off) % n_ch), device_id_type=MESH)

    loads = [pltpu.make_async_copy(a, b, load_sem.at[i]) for i, (a, b) in enumerate((
        (key_in, key), (value_in, value), (filt_in, filt), (table_in, table), (inverse_in, inverse), (query_in, query),
        (lags_in, lags)))]

    def own_copy(c):
        return pltpu.make_async_copy(
            cot.at[:, pl.ds(pl.multiple_of(core * rows + c * WIDE, WIDE), WIDE)],
            blocks.at[c, ch, pl.ds(own, tokens)], own_sem.at[c])

    def swap_copy(c):
        return remote(
            cot.at[:, pl.ds(pl.multiple_of((1 - core) * rows + c * WIDE, WIDE), WIDE)],
            blocks.at[c, ch, pl.ds(own, tokens)], swap_sem.at[0, c], swap_sem.at[1, c], (other, ch))

    def w_rows(c, q):
        return weights.at[c, pl.ds(pl.multiple_of(q * WIDE, WIDE), WIDE)]

    def w_piece(c):
        return weight.at[pl.ds(pl.multiple_of(c * WIDE, WIDE), WIDE)]

    w_own = [pltpu.make_async_copy(w_piece(c), w_rows(c, chip), load_sem.at[len(loads) + c]) for c in range(chunks)]

    def w1x(c):
        return remote(w_piece(c), w_rows(c, chip), w1_send.at[c, 0], w1_recv.at[c, 0], device(x_chip))

    def w1y(c, o):
        return remote(w_piece(c), w_rows(c, chip), w1_send.at[c, o], w1_recv.at[c, o], device(y_at(o) * 2 + x))

    def w2y(c, o):
        piece = weights.at[c, pl.ds(pl.multiple_of(x_chip * WIDE, wh), wh)]
        return remote(piece, piece, w2_send.at[c, ny - 1 + o], w2_recv.at[c, ny - 1 + o], device(y_at(o) * 2 + x))

    def w2x(c, o):
        piece = weights.at[c, pl.ds(pl.multiple_of((y_at(ny - o) * 2 + x) * WIDE + wh, wh), wh)]
        return remote(piece, piece, w2_send.at[c, o], w2_recv.at[c, o], device(x_chip))

    def z_copy(c, h, way):
        if way == 0:
            block, to = ch - h, ch + 1
        else:
            block, to = ch + h, ch - 1
        block = jnp.clip(block, 0, n_ch - 1)
        return remote(blocks.at[c, block], blocks.at[c, block], z_send.at[c, h, way], z_recv.at[c, h, way],
                      (ctx, jnp.clip(to, 0, n_ch - 1)))

    def sends(h, way):
        if way == 0:
            return jnp.logical_and(ch >= h, ch < n_ch - 1)
        return jnp.logical_and(ch + h < n_ch, ch > 0)

    def receives(h, way):
        if way == 0:
            return ch - 1 - h >= 0
        return ch + 1 + h < n_ch

    def z_start(c, h):
        for way in range(2):
            @pl.when(sends(h, way))
            def _():
                z_copy(c, h, way).start()

    def z_arrive(c, h):
        for way in range(2):
            @pl.when(receives(h, way))
            def _():
                z_copy(c, h, way).wait_recv()
        if h + 1 < hops:
            z_start(c, h + 1)

    before = remote(prodx.at[pl.ds(tokens, TAPS)], prodx.at[pl.ds(0, TAPS)], halo_sem.at[0], halo_sem.at[1],
                    (jnp.minimum(ctx + 1, n_ctx - 1), ch))
    after = remote(gatex.at[pl.ds(0, TAPS)], gatex.at[pl.ds(tokens, TAPS)], halo_sem.at[2], halo_sem.at[3],
                   (jnp.maximum(ctx - 1, 0), ch))
    gated_copy = remote(gated.at[pl.ds(own, tokens)], gated.at[pl.ds(own, tokens)], pair_sem.at[0, 0], pair_sem.at[1, 0],
                        (other, ch))

    def acc_copy(t):
        there = pl.ds(pl.multiple_of(theirs + t * TILE, TILE), TILE)
        return remote(acc.at[there], acc_in.at[pl.ds(pl.multiple_of(t * TILE, TILE), TILE)],
                      pair_sem.at[2, t], pair_sem.at[3, t], (other, ch))

    wide_tile = min(COLUMNS, channels)
    tiles = channels // wide_tile

    def columns(t):
        return pl.ds(pl.multiple_of(t * wide_tile, wide_tile), wide_tile)

    def key_store(t):
        return pltpu.make_async_copy(s_key.at[:, columns(t)], g_key.at[:, columns(t)], store_sem.at[0, t])

    def value_store(t):
        return pltpu.make_async_copy(s_value.at[:, columns(t)], g_value.at[:, columns(t)], store_sem.at[1, t])

    def query_store(t):
        at = pl.ds(pl.multiple_of(t * TAPS, TAPS), TAPS)
        return pltpu.make_async_copy(s_query.at[at], g_query.at[at], store_sem.at[2, t])

    def proj_store(c):
        place = pl.ds(pl.multiple_of(c * WIDE, WIDE), WIDE)
        return pltpu.make_async_copy(s_proj.at[c % 2], g_proj.at[place], proj_sem.at[c])

    filter_store = pltpu.make_async_copy(s_filter, g_filter, store_sem.at[3, 0])

    def a1(c):
        return remote(a1_out.at[c % 2], a1_in.at[c], a1_send.at[c], a1_recv.at[c], device(x_chip))

    def b1(c, o):
        return remote(b1_out.at[c % 2, o - 1], b1_in.at[c, o - 1], b1_send.at[c, o - 1], b1_recv.at[c, o - 1],
                      device(y_at(o) * 2 + x))

    def a2(c, o):
        return remote(a2_out.at[c % 2, o - 1], a2_in.at[c, o - 1], a2_send.at[c, o - 1], a2_recv.at[c, o - 1],
                      device(y_at(o) * 2 + x))

    def b2(c):
        return remote(b2_out.at[c % 2], b2_in.at[c], b2_send.at[c], b2_recv.at[c], device(x_chip))

    def part(c, target, side):
        return lax.dot_general(
            blocks[c, target], gated[:, side * half : (side + 1) * half], (((0,), (0,)), ((), ())),
            preferred_element_type=F32)

    def phase1(c):
        @pl.when(c >= 2)
        def _():
            a1(c - 2).wait_send()
            for o in range(1, ny):
                b1(c - 2, o).wait_send()

        for ky in range(ny):
            a1_out[c % 2, ky] = part(c, ky * 2 + 1 - x, 0).astype(BF16)
        a1(c).start()
        for o in range(1, ny):
            for kx in range(2):
                b1_out[c % 2, o - 1, kx] = part(c, y_at(o) * 2 + kx, 1).astype(BF16)
            b1(c, o).start()

    def phase2(c):
        @pl.when(c >= 2)
        def _():
            b2(c - 2).wait_send()
            for o in range(1, ny):
                a2(c - 2, o).wait_send()

        a1(c).wait_recv()
        for o in range(1, ny):
            ky = y_at(o)
            a2_out[c % 2, o - 1] = (part(c, ky * 2 + x, 0) + a1_in[c, ky].astype(F32)).astype(BF16)
            a2(c, o).start()
        total = part(c, x_chip, 1)
        for o in range(1, ny):
            b1(c, o).wait_recv()
            total += b1_in[c, o - 1, 1 - x].astype(F32)
        b2_out[c % 2] = total.astype(BF16)
        b2(c).start()

    def phase3(c):
        @pl.when(c >= 2)
        def _():
            proj_store(c - 2).wait()

        left = part(c, chip, 0) + a1_in[c, y].astype(F32)
        for o in range(1, ny):
            a2(c, o).wait_recv()
            left += a2_in[c, o - 1].astype(F32)
        s_proj[c % 2, :, :half] = left
        right = part(c, chip, 1)
        for o in range(1, ny):
            right += b1_in[c, o - 1, x].astype(F32)
        b2(c).wait_recv()
        s_proj[c % 2, :, half:] = right + b2_in[c].astype(F32)
        proj_store(c).start()

    def mix_chunk(c):
        for o in range(1, ny):
            w2y(c, o).wait_recv()
            w2x(c, o).wait_recv()

        for first in (theirs, own):
            @pl.loop(0, tokens // TILE)
            def _(i):
                at = pl.ds(pl.multiple_of(first + i * TILE, TILE), TILE)
                left = jnp.concatenate([blocks[c, q, at, :] for q in range(n_ch)], 1)
                acc[at, :] += dot32(left, weights[c])
                if first is theirs:
                    @pl.when(c == chunks - 1)
                    def _():
                        acc_copy(i).start()

    for load in loads[:2]:
        load.start()
    for c in range(chunks):
        own_copy(c).start()
    for load in loads[2:]:
        load.start()
    for load in w_own:
        load.start()
    pl.semaphore_wait(barrier, n_ctx + 1)

    @pl.loop(0, chunks)
    def _(c):
        swap_copy(c).start()

    def w_start(c):
        w1x(c).start()
        for o in range(1, ny):
            w1y(c, o).start()

    def w_arrive(c):
        w1x(c).wait_recv()
        for o in range(1, ny):
            w2y(c, o).start()
        for o in range(1, ny):
            w1y(c, o).wait_recv()
            w2x(c, o).start()

    def product(j):
        at = pl.ds(pl.multiple_of(j * TAPS, TAPS), TAPS)
        prodx[pl.ds(pl.multiple_of(j * TAPS + TAPS, TAPS), TAPS), :] = (
            key[at, :].astype(F32) * value[at, :].astype(F32)).astype(BF16)

    for load in loads[:2]:
        load.wait()
    product(tokens // TAPS - 1)

    @pl.when(ctx < n_ctx - 1)
    def _():
        before.start()

    @pl.loop(0, min(4, chunks))
    def _(c):
        w_start(c)

    @pl.loop(0, chunks)
    def _(c):
        own_copy(c).wait()
        swap_copy(c).wait_recv()

        @pl.when(c < AHEAD)
        def _():
            z_start(c, 0)

    pl.loop(0, tokens // TAPS - 1)(product)

    @pl.when(ctx == 0)
    def _():
        prodx[:TAPS, :] = jnp.zeros((TAPS, channels), BF16)

    acc[...] = jnp.zeros_like(acc)
    for load in loads[2:]:
        load.wait()

    @pl.when(ctx > 0)
    def _():
        before.wait_recv()

    @pl.loop(0, tiles)
    def _(i):
        at = columns(i)
        f = filt[at, :]
        f_spec = lax.dot_general(table[:, : 2 * TAPS], jnp.concatenate([f, f], 1), (((1,), (1,)), ((), ())),
                                 preferred_element_type=F32)
        fspec[:, at] = f_spec
        p_spec = forward(table[...], prodx[:, at])
        pspec[:, at] = p_spec
        mixed = backward(inverse[TAPS:, :], times(p_spec, f_spec))
        mix[:, at] = mixed
        gated[pl.ds(own, tokens), at] = (query[:, at].astype(F32) * mixed).astype(BF16)

    gated_copy.start()

    for load in w_own:
        load.wait()

    @pl.loop(0, min(2, chunks))
    def _(c):
        w_arrive(c)

    gated_copy.wait_recv()
    close = max(chunks - 3, 1)

    def sent(c):
        return jnp.where(c < close, jnp.maximum(c - 1, 0), c)

    def mixed_up_to(c):
        return jnp.where(c < close, c, c + 1)

    @pl.loop(0, chunks)
    def _(c):
        z_arrive(c, 0)

        @pl.when(c + 2 < chunks)
        def _():
            w_arrive(c + 2)

        @pl.when(c + 4 < chunks)
        def _():
            w_start(c + 4)

        for h in range(1, hops - 1):
            z_arrive(c, h)

        @pl.when(jnp.logical_and(c + 1 >= AHEAD, c + 1 < chunks))
        def _():
            z_start(c + 1, 0)

        pl.loop(sent(c - 1), sent(c))(phase2)
        pl.loop(sent(c - 2), sent(c - 1))(phase3)
        z_arrive(c, hops - 1)
        phase1(c)
        pl.loop(jnp.maximum(mixed_up_to(c - 1), 0), mixed_up_to(c))(mix_chunk)

    last = chunks - 1

    @pl.loop(0, tokens // TAPS)
    def _(i):
        @pl.when(i % (TILE // TAPS) == 0)
        def _():
            acc_copy(i // (TILE // TAPS)).wait_recv()

        at = pl.ds(pl.multiple_of(i * TAPS, TAPS), TAPS)
        grad_mix = acc[pl.ds(pl.multiple_of(own + i * TAPS, TAPS), TAPS), :] + acc_in[at, :]
        gatex[at, :] = (grad_mix * query[at, :].astype(F32)).astype(BF16)

        @pl.when(jnp.logical_and(i == 0, ctx > 0))
        def _():
            after.start()

        s_query[at, :] = (grad_mix * mix[at, :]).astype(BF16)
        query_store(i).start()

    @pl.when(ctx == n_ctx - 1)
    def _():
        gatex[tokens:, :] = jnp.zeros((TAPS, channels), BF16)

    share = channels // n_ctx

    def piece(i):
        return pl.ds(pl.multiple_of(i * share, share), share)

    def scatter(off):
        peer = (ctx + off) % n_ctx
        return remote(f_out.at[piece(peer)], f_in.at[off - 1], fs_send.at[off - 1], fs_recv.at[off - 1], (peer, ch))

    def gather(off, source):
        return remote(f_all.at[piece(source)], f_all.at[piece(source)], fg_send.at[off - 1], fg_recv.at[off - 1],
                      ((ctx + off) % n_ctx, ch))

    def filter_tile(i):
        at = columns(i)
        own_spec = forward(table[:, : 2 * tokens], gatex[:tokens, at])
        taps = backward(lags[...], times_conj(pspec[:, at], own_spec))
        pspec[:, at] = own_spec
        taps = taps.T
        s_filter[at, :] = taps
        f_out[at, :] = taps.astype(BF16)
        for p in range(wide_tile // share):
            owner = i * (wide_tile // share) + p

            @pl.when(owner != ctx)
            def _():
                scatter((owner - ctx + n_ctx) % n_ctx).start()

    def input_tile(i):
        at = columns(i)
        gate_spec = pspec[:, at] + forward(table[:, 2 * tokens :], gatex[tokens:, at])
        grad_prod = backward(inverse[:tokens, :], times_conj(gate_spec, fspec[:, at]))
        s_key[:, at] = (grad_prod * value[:, at].astype(F32)).astype(BF16)
        s_value[:, at] = (grad_prod * key[:, at].astype(F32)).astype(BF16)
        key_store(i).start()
        value_store(i).start()

    pl.loop(0, tiles)(filter_tile)
    phase2(last)
    phase3(last - 1)

    @pl.when(ctx < n_ctx - 1)
    def _():
        after.wait_recv()

    pl.loop(0, tiles // 2)(input_tile)
    total = s_filter[piece(ctx), :]
    for off in range(1, n_ctx):
        scatter(off).wait_recv()
        total += f_in[off - 1].astype(F32)
    f_all[piece(ctx), :] = total.astype(BF16)

    @pl.loop(1, n_ctx)
    def _(off):
        gather(off, ctx).start()

    pl.loop(tiles // 2, tiles)(input_tile)
    phase3(last)

    @pl.loop(1, n_ctx)
    def _(off):
        gather(off, (ctx + n_ctx - off) % n_ctx).wait_recv()

    s_filter[...] = f_all[...].astype(F32)
    filter_store.start()

    @pl.loop(1, n_ctx)
    def _(off):
        gather(off, ctx).wait_send()
        scatter(off).wait_send()

    @pl.when(ctx < n_ctx - 1)
    def _():
        before.wait_send()

    @pl.when(ctx > 0)
    def _():
        after.wait_send()

    gated_copy.wait_send()
    filter_store.wait()

    @pl.loop(0, tokens // TILE)
    def _(i):
        acc_copy(i).wait_send()

    @pl.loop(0, tokens // TAPS)
    def _(i):
        query_store(i).wait()

    @pl.loop(0, tiles)
    def _(i):
        key_store(i).wait()
        value_store(i).wait()

    for c in (last - 1, last):
        proj_store(c).wait()

    @pl.loop(0, chunks)
    def _(c):
        swap_copy(c).wait_send()
        w1x(c).wait_send()
        for o in range(1, ny):
            w1y(c, o).wait_send()
            w2y(c, o).wait_send()
            w2x(c, o).wait_send()
        for h in range(hops):
            for way in range(2):
                @pl.when(sends(h, way))
                def _():
                    z_copy(c, h, way).wait_send()

    for c in (last - 1, last):
        a1(c).wait_send()
        b2(c).wait_send()
        for o in range(1, ny):
            b1(c, o).wait_send()
            a2(c, o).wait_send()


PIECES = 2


def hand_over_kernel(n, *refs):
    ins, outs, held = refs[:n], refs[n : 2 * n], refs[2 * n : 3 * n]
    in_sem, out_sem = refs[3 * n :]
    steps = []
    for i in range(n):
        size = ins[i].shape[0] // PIECES
        for p in range(PIECES):
            at = pl.ds(p * size, size)
            steps.append((pltpu.make_async_copy(ins[i].at[at], held[i].at[at], in_sem.at[i, p]),
                          pltpu.make_async_copy(held[i].at[at], outs[i].at[at], out_sem.at[i, p])))
    for read, _ in steps:
        read.start()
    for read, write in steps:
        read.wait()
        write.start()
    for _, write in steps:
        write.wait()


def hand_over(arrays):
    n = len(arrays)
    return tuple(pl.pallas_call(
        functools.partial(hand_over_kernel, n),
        out_shape=tuple(jax.ShapeDtypeStruct(a.shape, a.dtype) for a in arrays),
        in_specs=[pl.BlockSpec(memory_space=pl.ANY)] * n,
        out_specs=[pl.BlockSpec(memory_space=pl.ANY)] * n,
        scratch_shapes=[pltpu.VMEM(a.shape, a.dtype) for a in arrays]
        + [pltpu.SemaphoreType.DMA((n, PIECES))] * 2,
        compiler_params=pltpu.CompilerParams(vmem_limit_bytes=62 * 2**20),
    )(*arrays))


def shards(query_act, key_act, value_act, filters, proj_weight, cotangent):
    n_ctx, n_ch = lax.axis_size("ctx"), lax.axis_size("ch")
    tokens, channels = query_act.shape
    rows = proj_weight.shape[0]
    assert n_ctx == 2 * n_ch and cotangent.shape[1] == 2 * rows
    chunks, ny, hops = rows // WIDE, n_ctx // 4, n_ch - 1
    points = tokens + TAPS
    half, share = channels // 2, channels // n_ctx
    table = basis(points)
    inverse = (table.T / (points // 2)).astype(np.float32)
    lags = inverse[TAPS - np.arange(TAPS)]
    tables = [jnp.asarray(t) for t in (pair_columns(table), triple_columns(inverse), triple_columns(lags))]
    dma = pltpu.SemaphoreType.DMA
    vmem = pltpu.VMEM
    outs = pl.pallas_call(
        functools.partial(kernel, n_ctx, n_ch),
        out_shape=(
            jax.ShapeDtypeStruct((tokens, channels), BF16),
            jax.ShapeDtypeStruct((tokens, channels), BF16),
            jax.ShapeDtypeStruct((tokens, channels), BF16),
            jax.ShapeDtypeStruct((channels, TAPS), F32),
            jax.ShapeDtypeStruct((rows, channels), F32),
        ),
        in_specs=[pl.BlockSpec(memory_space=pl.ANY)] * 9,
        out_specs=[pl.BlockSpec(memory_space=pl.ANY)] * 5,
        scratch_shapes=[
            vmem((chunks, n_ch, 2 * tokens, WIDE), BF16),
            vmem((chunks, n_ch * WIDE, channels), BF16),
            vmem((2 * tokens, channels), F32),
            vmem((tokens, channels), F32),
            vmem((tokens, channels), BF16),
            vmem((tokens, channels), BF16),
            vmem((tokens, channels), BF16),
            vmem((channels, TAPS), BF16),
            vmem((points, 2 * points), BF16),
            vmem((points, 3 * points), BF16),
            vmem((TAPS, 3 * points), BF16),
            vmem((points, channels), BF16),
            vmem((points, channels), BF16),
            vmem((2 * tokens, channels), BF16),
            vmem((tokens, channels), F32),
            vmem((points, channels), F32),
            vmem((points, channels), F32),
            vmem((2, ny, WIDE, half), BF16),
            vmem((2, ny - 1, 2, WIDE, half), BF16),
            vmem((2, ny - 1, WIDE, half), BF16),
            vmem((2, WIDE, half), BF16),
            vmem((chunks, ny, WIDE, half), BF16),
            vmem((chunks, ny - 1, 2, WIDE, half), BF16),
            vmem((chunks, ny - 1, WIDE, half), BF16),
            vmem((chunks, WIDE, half), BF16),
            vmem((channels, TAPS), BF16),
            vmem((n_ctx - 1, share, TAPS), BF16),
            vmem((channels, TAPS), BF16),
            vmem((tokens, channels), BF16),
            vmem((tokens, channels), BF16),
            vmem((tokens, channels), BF16),
            vmem((channels, TAPS), F32),
            vmem((2, WIDE, channels), F32),
            dma((4, max(channels // TILE, tokens // TAPS))),
            dma((chunks,)),
            dma((7 + chunks,)),
            dma((chunks,)),
            dma((2, chunks)),
            dma((chunks, hops, 2)),
            dma((chunks, hops, 2)),
            dma((chunks, ny)),
            dma((chunks, ny)),
            dma((chunks, 2 * ny)),
            dma((chunks, 2 * ny)),
            dma((chunks,)),
            dma((chunks,)),
            dma((chunks, ny - 1)),
            dma((chunks, ny - 1)),
            dma((chunks, ny - 1)),
            dma((chunks, ny - 1)),
            dma((chunks,)),
            dma((chunks,)),
            dma((4,)),
            dma((4, tokens // TILE)),
            dma((n_ctx - 1,)),
            dma((n_ctx - 1,)),
            dma((n_ctx - 1,)),
            dma((n_ctx - 1,)),
        ],
        compiler_params=pltpu.CompilerParams(
            collective_id=0, has_side_effects=True, vmem_limit_bytes=63 * 2**20
        ),
    )(query_act, key_act, value_act, filters, proj_weight, cotangent, *tables)
    return hand_over(outs)


def solution(mesh):
    return jax.shard_map(
        shards,
        mesh=mesh,
        in_specs=(
            P("ctx", "ch"),
            P("ctx", "ch"),
            P("ctx", "ch"),
            P("ch", None),
            P("ctx", "ch"),
            P("ctx", "ch"),
        ),
        out_specs=(P("ctx", "ch"), P("ctx", "ch"), P("ctx", "ch"), P("ch", None), P("ctx", "ch")),
        check_vma=False,
    )
```

```python
import functools

import jax
import jax.numpy as jnp
import ml_dtypes
import numpy as np
from jax import lax
from jax.experimental import pallas as pl
from jax.experimental.pallas import tpu as pltpu
from jax.sharding import PartitionSpec as P

TAPS = 128
WIDE = 128
TILE = 256
COLUMNS = 512
AHEAD = 3
MESH = pl.DeviceIdType.MESH
BF16 = jnp.bfloat16
F32 = jnp.float32


def basis(points):
    freqs = points // 2
    phase = (2 * np.arange(freqs)[:, None] + 1) * np.arange(points)[None, :] % (2 * points)
    angle = np.pi * phase / points
    return np.concatenate([np.cos(angle), np.sin(angle)], 0).astype(np.float32)


def constant_pair(a):
    hi = a.astype(ml_dtypes.bfloat16)
    lo = (a - hi.astype(np.float32)).astype(ml_dtypes.bfloat16)
    return hi, lo


def split(a):
    hi = a.astype(BF16)
    return hi, (a - hi.astype(F32)).astype(BF16)


def dot32(a, b):
    return jnp.dot(a, b, preferred_element_type=F32)


def pair_columns(a):
    hi, lo = constant_pair(a)
    blocks = [t[:, i : i + TAPS] for i in range(0, a.shape[1], TAPS) for t in (hi, lo)]
    return np.concatenate(blocks, 1)


def triple_columns(a):
    hi, lo = constant_pair(a)
    return np.concatenate([hi, hi, lo], 1)


def forward(table, x):
    blocks = [x[i : i + TAPS] for i in range(0, x.shape[0], TAPS) for _ in range(2)]
    return dot32(table, jnp.concatenate(blocks, 0))


def backward(table, y):
    hi, lo = split(y)
    return dot32(table, jnp.concatenate([hi, lo, hi], 0))


def halves(x):
    n = x.shape[0] // 2
    return x[:n], x[n:]


def times(x, f):
    (xc, xs), (fc, fs) = halves(x), halves(f)
    return jnp.concatenate([xc * fc - xs * fs, xc * fs + xs * fc], 0)


def times_conj(x, f):
    (xc, xs), (fc, fs) = halves(x), halves(f)
    return jnp.concatenate([xc * fc + xs * fs, xs * fc - xc * fs], 0)


def kernel(n_ctx, n_ch, query_in, key_in, value_in, filt_in, weight, cot, table_in, inverse_in, lags_in,
           g_query, g_key, g_value, g_filter, g_proj,
           blocks, weights, acc, acc_in, query, key, value, filt, table, inverse, lags,
           prodx, gatex, gated, mix, pspec, fspec,
           a1_out, b1_out, a2_out, b2_out, a1_in, b1_in, a2_in, b2_in, f_out, f_in, f_all,
           s_query, s_key, s_value, s_filter, s_proj, store_sem, proj_sem,
           load_sem, own_sem, swap_sem, z_send, z_recv, w1_send, w1_recv, w2_send, w2_recv,
           a1_send, a1_recv, b1_send, b1_recv, a2_send, a2_recv, b2_send, b2_recv,
           halo_sem, pair_sem, fs_send, fs_recv, fg_send, fg_recv):
    chips = n_ctx // 2
    ny = chips // 2
    hops = n_ch - 1
    ctx = lax.axis_index("ctx")
    ch = lax.axis_index("ch")
    chip, core = ctx // 2, ctx % 2
    y, x = chip // 2, chip % 2
    other = chip * 2 + 1 - core
    x_chip = y * 2 + 1 - x
    tokens = query.shape[0]
    channels = query.shape[1]
    rows = weight.shape[0]
    chunks = rows // WIDE
    half = channels // 2
    wh = WIDE // 2
    own = pl.multiple_of(core * tokens, tokens)
    theirs = pl.multiple_of((1 - core) * tokens, tokens)

    def device(c):
        return (c * 2 + core, ch)

    def y_at(o):
        return (y + o) % ny

    def remote(src, dst, send, recv, to):
        return pltpu.make_async_remote_copy(src, dst, send, recv, device_id=to, device_id_type=MESH)

    barrier = pltpu.get_barrier_semaphore()
    for off in range(1, n_ctx):
        pl.semaphore_signal(barrier, inc=1, device_id=((ctx + off) % n_ctx, ch), device_id_type=MESH)
    for off in (1, n_ch - 1):
        pl.semaphore_signal(barrier, inc=1, device_id=(ctx, (ch + off) % n_ch), device_id_type=MESH)

    loads = [pltpu.make_async_copy(a, b, load_sem.at[i]) for i, (a, b) in enumerate((
        (key_in, key), (value_in, value), (filt_in, filt), (table_in, table), (inverse_in, inverse), (query_in, query),
        (lags_in, lags)))]

    def own_copy(c):
        return pltpu.make_async_copy(
            cot.at[:, pl.ds(pl.multiple_of(core * rows + c * WIDE, WIDE), WIDE)],
            blocks.at[c, ch, pl.ds(own, tokens)], own_sem.at[c])

    def swap_copy(c):
        return remote(
            cot.at[:, pl.ds(pl.multiple_of((1 - core) * rows + c * WIDE, WIDE), WIDE)],
            blocks.at[c, ch, pl.ds(own, tokens)], swap_sem.at[0, c], swap_sem.at[1, c], (other, ch))

    def w_rows(c, q):
        return weights.at[c, pl.ds(pl.multiple_of(q * WIDE, WIDE), WIDE)]

    def w_piece(c):
        return weight.at[pl.ds(pl.multiple_of(c * WIDE, WIDE), WIDE)]

    w_own = [pltpu.make_async_copy(w_piece(c), w_rows(c, chip), load_sem.at[len(loads) + c]) for c in range(chunks)]

    def w1x(c):
        return remote(w_piece(c), w_rows(c, chip), w1_send.at[c, 0], w1_recv.at[c, 0], device(x_chip))

    def w1y(c, o):
        return remote(w_piece(c), w_rows(c, chip), w1_send.at[c, o], w1_recv.at[c, o], device(y_at(o) * 2 + x))

    def w2y(c, o):
        piece = weights.at[c, pl.ds(pl.multiple_of(x_chip * WIDE, wh), wh)]
        return remote(piece, piece, w2_send.at[c, ny - 1 + o], w2_recv.at[c, ny - 1 + o], device(y_at(o) * 2 + x))

    def w2x(c, o):
        piece = weights.at[c, pl.ds(pl.multiple_of((y_at(ny - o) * 2 + x) * WIDE + wh, wh), wh)]
        return remote(piece, piece, w2_send.at[c, o], w2_recv.at[c, o], device(x_chip))

    def z_copy(c, h, way):
        if way == 0:
            block, to = ch - h, ch + 1
        else:
            block, to = ch + h, ch - 1
        block = jnp.clip(block, 0, n_ch - 1)
        return remote(blocks.at[c, block], blocks.at[c, block], z_send.at[c, h, way], z_recv.at[c, h, way],
                      (ctx, jnp.clip(to, 0, n_ch - 1)))

    def sends(h, way):
        if way == 0:
            return jnp.logical_and(ch >= h, ch < n_ch - 1)
        return jnp.logical_and(ch + h < n_ch, ch > 0)

    def receives(h, way):
        if way == 0:
            return ch - 1 - h >= 0
        return ch + 1 + h < n_ch

    def z_start(c, h):
        for way in range(2):
            @pl.when(sends(h, way))
            def _():
                z_copy(c, h, way).start()

    def z_arrive(c, h):
        for way in range(2):
            @pl.when(receives(h, way))
            def _():
                z_copy(c, h, way).wait_recv()
        if h + 1 < hops:
            z_start(c, h + 1)

    before = remote(prodx.at[pl.ds(tokens, TAPS)], prodx.at[pl.ds(0, TAPS)], halo_sem.at[0], halo_sem.at[1],
                    (jnp.minimum(ctx + 1, n_ctx - 1), ch))
    after = remote(gatex.at[pl.ds(0, TAPS)], gatex.at[pl.ds(tokens, TAPS)], halo_sem.at[2], halo_sem.at[3],
                   (jnp.maximum(ctx - 1, 0), ch))
    gated_copy = remote(gated.at[pl.ds(own, tokens)], gated.at[pl.ds(own, tokens)], pair_sem.at[0, 0], pair_sem.at[1, 0],
                        (other, ch))

    def acc_copy(t):
        there = pl.ds(pl.multiple_of(theirs + t * TILE, TILE), TILE)
        return remote(acc.at[there], acc_in.at[pl.ds(pl.multiple_of(t * TILE, TILE), TILE)],
                      pair_sem.at[2, t], pair_sem.at[3, t], (other, ch))

    wide_tile = min(COLUMNS, channels)
    tiles = channels // wide_tile

    def columns(t):
        return pl.ds(pl.multiple_of(t * wide_tile, wide_tile), wide_tile)

    def key_store(t):
        return pltpu.make_async_copy(s_key.at[:, columns(t)], g_key.at[:, columns(t)], store_sem.at[0, t])

    def value_store(t):
        return pltpu.make_async_copy(s_value.at[:, columns(t)], g_value.at[:, columns(t)], store_sem.at[1, t])

    def query_store(t):
        at = pl.ds(pl.multiple_of(t * TAPS, TAPS), TAPS)
        return pltpu.make_async_copy(s_query.at[at], g_query.at[at], store_sem.at[2, t])

    def proj_store(c):
        place = pl.ds(pl.multiple_of(c * WIDE, WIDE), WIDE)
        return pltpu.make_async_copy(s_proj.at[c % 2], g_proj.at[place], proj_sem.at[c])

    filter_store = pltpu.make_async_copy(s_filter, g_filter, store_sem.at[3, 0])

    def a1(c, ky):
        return remote(a1_out.at[c % 2, ky], a1_in.at[c, ky], a1_send.at[c, ky], a1_recv.at[c, ky], device(x_chip))

    def b1(c, o, kx):
        return remote(b1_out.at[c % 2, o - 1, kx], b1_in.at[c, o - 1, kx], b1_send.at[c, o - 1, kx],
                      b1_recv.at[c, o - 1, kx], device(y_at(o) * 2 + x))

    def first_sent(c):
        for ky in range(ny):
            a1(c, ky).wait_send()
        for o in range(1, ny):
            for kx in range(2):
                b1(c, o, kx).wait_send()

    def a2(c, o):
        return remote(a2_out.at[c % 2, o - 1], a2_in.at[c, o - 1], a2_send.at[c, o - 1], a2_recv.at[c, o - 1],
                      device(y_at(o) * 2 + x))

    def b2(c):
        return remote(b2_out.at[c % 2], b2_in.at[c], b2_send.at[c], b2_recv.at[c], device(x_chip))

    def part(c, target, side):
        return lax.dot_general(
            blocks[c, target], gated[:, side * half : (side + 1) * half], (((0,), (0,)), ((), ())),
            preferred_element_type=F32)

    def phase1(c, last_hop):
        def due(target):
            return (jnp.abs(target - ch) == hops) == last_hop

        if not last_hop:
            @pl.when(c >= 2)
            def _():
                first_sent(c - 2)

        for ky in range(ny):
            @pl.when(due(ky * 2 + 1 - x))
            def _():
                a1_out[c % 2, ky] = part(c, ky * 2 + 1 - x, 0).astype(BF16)
                a1(c, ky).start()
        for o in range(1, ny):
            for kx in range(2):
                @pl.when(due(y_at(o) * 2 + kx))
                def _():
                    b1_out[c % 2, o - 1, kx] = part(c, y_at(o) * 2 + kx, 1).astype(BF16)
                    b1(c, o, kx).start()

    def phase2(c):
        @pl.when(c >= 2)
        def _():
            b2(c - 2).wait_send()
            for o in range(1, ny):
                a2(c - 2, o).wait_send()

        for ky in range(ny):
            a1(c, ky).wait_recv()
        for o in range(1, ny):
            ky = y_at(o)
            a2_out[c % 2, o - 1] = (part(c, ky * 2 + x, 0) + a1_in[c, ky].astype(F32)).astype(BF16)
            a2(c, o).start()
        total = part(c, x_chip, 1)
        for o in range(1, ny):
            for kx in range(2):
                b1(c, o, kx).wait_recv()
            total += b1_in[c, o - 1, 1 - x].astype(F32)
        b2_out[c % 2] = total.astype(BF16)
        b2(c).start()

    def phase3(c):
        @pl.when(c >= 2)
        def _():
            proj_store(c - 2).wait()

        left = part(c, chip, 0) + a1_in[c, y].astype(F32)
        for o in range(1, ny):
            a2(c, o).wait_recv()
            left += a2_in[c, o - 1].astype(F32)
        s_proj[c % 2, :, :half] = left
        right = part(c, chip, 1)
        for o in range(1, ny):
            right += b1_in[c, o - 1, x].astype(F32)
        b2(c).wait_recv()
        s_proj[c % 2, :, half:] = right + b2_in[c].astype(F32)
        proj_store(c).start()

    def mix_chunk(c):
        for o in range(1, ny):
            w2y(c, o).wait_recv()
            w2x(c, o).wait_recv()

        for first in (theirs, own):
            @pl.loop(0, tokens // TILE)
            def _(i):
                at = pl.ds(pl.multiple_of(first + i * TILE, TILE), TILE)
                left = jnp.concatenate([blocks[c, q, at, :] for q in range(n_ch)], 1)
                acc[at, :] += dot32(left, weights[c])
                if first is theirs:
                    @pl.when(c == chunks - 1)
                    def _():
                        acc_copy(i).start()

    for load in loads[:2]:
        load.start()
    for c in range(chunks):
        own_copy(c).start()
    for load in loads[2:]:
        load.start()
    for load in w_own:
        load.start()
    pl.semaphore_wait(barrier, n_ctx + 1)

    @pl.loop(0, chunks)
    def _(c):
        swap_copy(c).start()

    def w_start(c):
        w1x(c).start()
        for o in range(1, ny):
            w1y(c, o).start()

    def w_arrive(c):
        w1x(c).wait_recv()
        for o in range(1, ny):
            w2y(c, o).start()
        for o in range(1, ny):
            w1y(c, o).wait_recv()
            w2x(c, o).start()

    def product(j):
        at = pl.ds(pl.multiple_of(j * TAPS, TAPS), TAPS)
        prodx[pl.ds(pl.multiple_of(j * TAPS + TAPS, TAPS), TAPS), :] = (
            key[at, :].astype(F32) * value[at, :].astype(F32)).astype(BF16)

    for load in loads[:2]:
        load.wait()
    product(tokens // TAPS - 1)

    @pl.when(ctx < n_ctx - 1)
    def _():
        before.start()

    @pl.loop(0, min(4, chunks))
    def _(c):
        w_start(c)

    @pl.loop(0, chunks)
    def _(c):
        own_copy(c).wait()
        swap_copy(c).wait_recv()

        @pl.when(c < AHEAD)
        def _():
            z_start(c, 0)

    pl.loop(0, tokens // TAPS - 1)(product)

    @pl.when(ctx == 0)
    def _():
        prodx[:TAPS, :] = jnp.zeros((TAPS, channels), BF16)

    acc[...] = jnp.zeros_like(acc)
    for load in loads[2:]:
        load.wait()

    @pl.when(ctx > 0)
    def _():
        before.wait_recv()

    @pl.loop(0, tiles)
    def _(i):
        at = columns(i)
        f = filt[at, :]
        f_spec = lax.dot_general(table[:, : 2 * TAPS], jnp.concatenate([f, f], 1), (((1,), (1,)), ((), ())),
                                 preferred_element_type=F32)
        fspec[:, at] = f_spec
        p_spec = forward(table[...], prodx[:, at])
        pspec[:, at] = p_spec
        mixed = backward(inverse[TAPS:, :], times(p_spec, f_spec))
        mix[:, at] = mixed
        gated[pl.ds(own, tokens), at] = (query[:, at].astype(F32) * mixed).astype(BF16)

    gated_copy.start()

    for load in w_own:
        load.wait()

    @pl.loop(0, min(2, chunks))
    def _(c):
        w_arrive(c)

    gated_copy.wait_recv()
    close = max(chunks - 3, 1)

    def sent(c):
        return jnp.where(c < close, jnp.maximum(c - 1, 0), c)

    def mixed_up_to(c):
        return jnp.where(c < close, c, c + 1)

    @pl.loop(0, chunks)
    def _(c):
        z_arrive(c, 0)

        @pl.when(c + 2 < chunks)
        def _():
            w_arrive(c + 2)

        @pl.when(c + 4 < chunks)
        def _():
            w_start(c + 4)

        for h in range(1, hops - 1):
            z_arrive(c, h)

        @pl.when(jnp.logical_and(c + 1 >= AHEAD, c + 1 < chunks))
        def _():
            z_start(c + 1, 0)

        pl.loop(sent(c - 1), sent(c))(phase2)
        pl.loop(sent(c - 2), sent(c - 1))(phase3)
        phase1(c, False)
        z_arrive(c, hops - 1)
        phase1(c, True)
        pl.loop(jnp.maximum(mixed_up_to(c - 1), 0), mixed_up_to(c))(mix_chunk)

    last = chunks - 1

    @pl.loop(0, tokens // TAPS)
    def _(i):
        @pl.when(i % (TILE // TAPS) == 0)
        def _():
            acc_copy(i // (TILE // TAPS)).wait_recv()

        at = pl.ds(pl.multiple_of(i * TAPS, TAPS), TAPS)
        grad_mix = acc[pl.ds(pl.multiple_of(own + i * TAPS, TAPS), TAPS), :] + acc_in[at, :]
        gatex[at, :] = (grad_mix * query[at, :].astype(F32)).astype(BF16)

        @pl.when(jnp.logical_and(i == 0, ctx > 0))
        def _():
            after.start()

        s_query[at, :] = (grad_mix * mix[at, :]).astype(BF16)
        query_store(i).start()

    @pl.when(ctx == n_ctx - 1)
    def _():
        gatex[tokens:, :] = jnp.zeros((TAPS, channels), BF16)

    share = channels // n_ctx

    def piece(i):
        return pl.ds(pl.multiple_of(i * share, share), share)

    def scatter(off):
        peer = (ctx + off) % n_ctx
        return remote(f_out.at[piece(peer)], f_in.at[off - 1], fs_send.at[off - 1], fs_recv.at[off - 1], (peer, ch))

    def gather(off, source):
        return remote(f_all.at[piece(source)], f_all.at[piece(source)], fg_send.at[off - 1], fg_recv.at[off - 1],
                      ((ctx + off) % n_ctx, ch))

    def filter_tile(i):
        at = columns(i)
        own_spec = forward(table[:, : 2 * tokens], gatex[:tokens, at])
        taps = backward(lags[...], times_conj(pspec[:, at], own_spec))
        pspec[:, at] = own_spec
        taps = taps.T
        s_filter[at, :] = taps
        f_out[at, :] = taps.astype(BF16)
        for p in range(wide_tile // share):
            owner = i * (wide_tile // share) + p

            @pl.when(owner != ctx)
            def _():
                scatter((owner - ctx + n_ctx) % n_ctx).start()

    def input_tile(i):
        at = columns(i)
        gate_spec = pspec[:, at] + forward(table[:, 2 * tokens :], gatex[tokens:, at])
        grad_prod = backward(inverse[:tokens, :], times_conj(gate_spec, fspec[:, at]))
        s_key[:, at] = (grad_prod * value[:, at].astype(F32)).astype(BF16)
        s_value[:, at] = (grad_prod * key[:, at].astype(F32)).astype(BF16)
        key_store(i).start()
        value_store(i).start()

    pl.loop(0, tiles)(filter_tile)
    phase2(last)
    phase3(last - 1)

    @pl.when(ctx < n_ctx - 1)
    def _():
        after.wait_recv()

    pl.loop(0, tiles // 2)(input_tile)
    total = s_filter[piece(ctx), :]
    for off in range(1, n_ctx):
        scatter(off).wait_recv()
        total += f_in[off - 1].astype(F32)
    f_all[piece(ctx), :] = total.astype(BF16)

    @pl.loop(1, n_ctx)
    def _(off):
        gather(off, ctx).start()

    pl.loop(tiles // 2, tiles)(input_tile)
    phase3(last)

    @pl.loop(1, n_ctx)
    def _(off):
        gather(off, (ctx + n_ctx - off) % n_ctx).wait_recv()

    s_filter[...] = f_all[...].astype(F32)
    filter_store.start()

    @pl.loop(1, n_ctx)
    def _(off):
        gather(off, ctx).wait_send()
        scatter(off).wait_send()

    @pl.when(ctx < n_ctx - 1)
    def _():
        before.wait_send()

    @pl.when(ctx > 0)
    def _():
        after.wait_send()

    gated_copy.wait_send()
    filter_store.wait()

    @pl.loop(0, tokens // TILE)
    def _(i):
        acc_copy(i).wait_send()

    @pl.loop(0, tokens // TAPS)
    def _(i):
        query_store(i).wait()

    @pl.loop(0, tiles)
    def _(i):
        key_store(i).wait()
        value_store(i).wait()

    for c in (last - 1, last):
        proj_store(c).wait()

    @pl.loop(0, chunks)
    def _(c):
        swap_copy(c).wait_send()
        w1x(c).wait_send()
        for o in range(1, ny):
            w1y(c, o).wait_send()
            w2y(c, o).wait_send()
            w2x(c, o).wait_send()
        for h in range(hops):
            for way in range(2):
                @pl.when(sends(h, way))
                def _():
                    z_copy(c, h, way).wait_send()

    for c in (last - 1, last):
        first_sent(c)
        b2(c).wait_send()
        for o in range(1, ny):
            a2(c, o).wait_send()


PIECES = 2


def hand_over_kernel(n, *refs):
    ins, outs, held = refs[:n], refs[n : 2 * n], refs[2 * n : 3 * n]
    in_sem, out_sem = refs[3 * n :]
    steps = []
    for i in range(n):
        size = ins[i].shape[0] // PIECES
        for p in range(PIECES):
            at = pl.ds(p * size, size)
            steps.append((pltpu.make_async_copy(ins[i].at[at], held[i].at[at], in_sem.at[i, p]),
                          pltpu.make_async_copy(held[i].at[at], outs[i].at[at], out_sem.at[i, p])))
    for read, _ in steps:
        read.start()
    for read, write in steps:
        read.wait()
        write.start()
    for _, write in steps:
        write.wait()


def hand_over(arrays):
    n = len(arrays)
    return tuple(pl.pallas_call(
        functools.partial(hand_over_kernel, n),
        out_shape=tuple(jax.ShapeDtypeStruct(a.shape, a.dtype) for a in arrays),
        in_specs=[pl.BlockSpec(memory_space=pl.ANY)] * n,
        out_specs=[pl.BlockSpec(memory_space=pl.ANY)] * n,
        scratch_shapes=[pltpu.VMEM(a.shape, a.dtype) for a in arrays]
        + [pltpu.SemaphoreType.DMA((n, PIECES))] * 2,
        compiler_params=pltpu.CompilerParams(vmem_limit_bytes=62 * 2**20),
    )(*arrays))


def shards(query_act, key_act, value_act, filters, proj_weight, cotangent):
    n_ctx, n_ch = lax.axis_size("ctx"), lax.axis_size("ch")
    tokens, channels = query_act.shape
    rows = proj_weight.shape[0]
    assert n_ctx == 2 * n_ch and cotangent.shape[1] == 2 * rows
    chunks, ny, hops = rows // WIDE, n_ctx // 4, n_ch - 1
    points = tokens + TAPS
    half, share = channels // 2, channels // n_ctx
    table = basis(points)
    inverse = (table.T / (points // 2)).astype(np.float32)
    lags = inverse[TAPS - np.arange(TAPS)]
    tables = [jnp.asarray(t) for t in (pair_columns(table), triple_columns(inverse), triple_columns(lags))]
    dma = pltpu.SemaphoreType.DMA
    vmem = pltpu.VMEM
    outs = pl.pallas_call(
        functools.partial(kernel, n_ctx, n_ch),
        out_shape=(
            jax.ShapeDtypeStruct((tokens, channels), BF16),
            jax.ShapeDtypeStruct((tokens, channels), BF16),
            jax.ShapeDtypeStruct((tokens, channels), BF16),
            jax.ShapeDtypeStruct((channels, TAPS), F32),
            jax.ShapeDtypeStruct((rows, channels), F32),
        ),
        in_specs=[pl.BlockSpec(memory_space=pl.ANY)] * 9,
        out_specs=[pl.BlockSpec(memory_space=pl.ANY)] * 5,
        scratch_shapes=[
            vmem((chunks, n_ch, 2 * tokens, WIDE), BF16),
            vmem((chunks, n_ch * WIDE, channels), BF16),
            vmem((2 * tokens, channels), F32),
            vmem((tokens, channels), F32),
            vmem((tokens, channels), BF16),
            vmem((tokens, channels), BF16),
            vmem((tokens, channels), BF16),
            vmem((channels, TAPS), BF16),
            vmem((points, 2 * points), BF16),
            vmem((points, 3 * points), BF16),
            vmem((TAPS, 3 * points), BF16),
            vmem((points, channels), BF16),
            vmem((points, channels), BF16),
            vmem((2 * tokens, channels), BF16),
            vmem((tokens, channels), F32),
            vmem((points, channels), F32),
            vmem((points, channels), F32),
            vmem((2, ny, WIDE, half), BF16),
            vmem((2, ny - 1, 2, WIDE, half), BF16),
            vmem((2, ny - 1, WIDE, half), BF16),
            vmem((2, WIDE, half), BF16),
            vmem((chunks, ny, WIDE, half), BF16),
            vmem((chunks, ny - 1, 2, WIDE, half), BF16),
            vmem((chunks, ny - 1, WIDE, half), BF16),
            vmem((chunks, WIDE, half), BF16),
            vmem((channels, TAPS), BF16),
            vmem((n_ctx - 1, share, TAPS), BF16),
            vmem((channels, TAPS), BF16),
            vmem((tokens, channels), BF16),
            vmem((tokens, channels), BF16),
            vmem((tokens, channels), BF16),
            vmem((channels, TAPS), F32),
            vmem((2, WIDE, channels), F32),
            dma((4, max(channels // TILE, tokens // TAPS))),
            dma((chunks,)),
            dma((7 + chunks,)),
            dma((chunks,)),
            dma((2, chunks)),
            dma((chunks, hops, 2)),
            dma((chunks, hops, 2)),
            dma((chunks, ny)),
            dma((chunks, ny)),
            dma((chunks, 2 * ny)),
            dma((chunks, 2 * ny)),
            dma((chunks, ny)),
            dma((chunks, ny)),
            dma((chunks, ny - 1, 2)),
            dma((chunks, ny - 1, 2)),
            dma((chunks, ny - 1)),
            dma((chunks, ny - 1)),
            dma((chunks,)),
            dma((chunks,)),
            dma((4,)),
            dma((4, tokens // TILE)),
            dma((n_ctx - 1,)),
            dma((n_ctx - 1,)),
            dma((n_ctx - 1,)),
            dma((n_ctx - 1,)),
        ],
        compiler_params=pltpu.CompilerParams(
            collective_id=0, has_side_effects=True, vmem_limit_bytes=63 * 2**20
        ),
    )(query_act, key_act, value_act, filters, proj_weight, cotangent, *tables)
    return hand_over(outs)


def solution(mesh):
    return jax.shard_map(
        shards,
        mesh=mesh,
        in_specs=(
            P("ctx", "ch"),
            P("ctx", "ch"),
            P("ctx", "ch"),
            P("ch", None),
            P("ctx", "ch"),
            P("ctx", "ch"),
        ),
        out_specs=(P("ctx", "ch"), P("ctx", "ch"), P("ctx", "ch"), P("ch", None), P("ctx", "ch")),
        check_vma=False,
    )
```
